256 devices in a mesh: ep: 64 (over y, z_lo, x), fsdp: 4 (over z_hi, core).
Axes of the slice: x: 4, y: 4, z: 8 (z_hi: 2, z_lo: 4; z = z_hi * 4 + z_lo), core: 2. Of those that a mesh axis runs over, the one named last changes fastest.
Arguments:
- tokens: bfloat16 [32768, 4096], P(('ep', 'fsdp')), may hold values from -6 to 6
- expert_ids: int32 [32768, 2], P(('ep', 'fsdp')), may hold values from 0 to 15, all different within a row; in each aligned block of 128 rows (0 to 127, 128 to 255, ...) at most 18 rows name the same one
- gate_probs: float32 [32768, 2], P(('ep', 'fsdp')), may hold values from 0.1 to 1
- w_up: bfloat16 [4096, 24576], P('fsdp', 'ep'), may hold values from -0.09375 to 0.09375
- w_down: bfloat16 [24576, 4096], P('ep', 'fsdp'), may hold values from -0.0546875 to 0.0546875
- cotangent: bfloat16 [32768, 4096], P(('ep', 'fsdp')), may hold values from -1.5 to 1.5
Outputs:
- grad_up: bfloat16 [4096, 24576], P('fsdp', 'ep')
- grad_down: bfloat16 [24576, 4096], P('ep', 'fsdp')
The draws below stay inside these ranges and needn't reach their ends.
Inputs may be any that keep to these rules, and one draw needn't show every extreme that they name: `expert_ids`: the 2 ids of a token differ. In each aligned block of 128 rows (the rows of one device) no id is named by more than 18 rows.
All inputs are finite; a program needn't handle non-finite values.
Results may differ from the reference program's by a relative error of at most 0.02.
Values may be sent and summed in bfloat16 or wider, within the bound.
No kernel may reach another device: no remote copies, remote signals or barrier semaphores. Data moves between devices by JAX's collectives and lax.ppermute only.
A program may use at most 192 MiB of HBM per device.

```python
import math
import jax
import jax.numpy as jnp
import numpy as np
from jax import lax

D = 4096
EXPERTS = 16
TOP = 2
TOK_DEV = 128
CAP = 18
TOKENS = 32768
FFW = 12288
FF_ALL = 24576
N_EP = 64
N_FSDP = 4


def levels(stream_key, extent, pieces, least, largest):
    def one(axis_at, shards_of):
        draws = jax.random.uniform(jax.random.fold_in(jax.random.fold_in(stream_key, 6), axis_at), (shards_of,), jnp.float32, least / len(pieces), largest / len(pieces))
        return jnp.repeat(jnp.exp(draws), extent[axis_at] // shards_of).reshape((-1,) + (1,) * (len(extent) - axis_at - 1))

    loudness = one(*pieces[0])
    for cut in pieces[1:]:
        loudness = loudness * one(*cut)
    return loudness


def shared_out(stream_key, own, number, rows, amount, top, reach, skew):
    ranking = jax.random.permutation(stream_key, amount)
    heavy_load, ordinary = load_shares(amount, rows * top, reach, skew, True), load_shares(amount, rows * top, reach, skew, False)
    places = jnp.arange(amount)

    def named(tallies, offset_by):
        used = int((tallies > 0).sum())
        fixed = max(1, used // 4)
        passed = fixed + (places - fixed + offset_by * (used - fixed)) % max(1, amount - fixed)
        return jnp.zeros((amount,), jnp.int32).at[ranking[jnp.where(places < fixed, places, passed)]].set(jnp.asarray(tallies, jnp.int32))

    tallies = jnp.where(number % 4 == 0, named(heavy_load, number // 4), named(ordinary, number - number // 4 - 1))
    mixed = jax.random.permutation(jax.random.fold_in(own, 3), amount)
    giver, receiver = mixed[0:amount // 2 * 2:2], mixed[1:amount // 2 * 2:2]
    margin = jnp.minimum(tallies[giver] - 1, reach - tallies[receiver]) // 2
    margin = jnp.where((giver == ranking[0]) | (receiver == ranking[0]) | (tallies[receiver] == 0), 0, jnp.maximum(margin, 0))
    passed = jax.random.randint(jax.random.fold_in(own, 4), (amount // 2,), 0, 1 << 20) % (margin + 1)
    tallies = tallies.at[giver].add(-passed).at[receiver].add(passed)
    items = jnp.searchsorted(jnp.cumsum(tallies), jnp.arange(rows * top), side="right").astype(jnp.int32)
    table = items.reshape(top, rows).T
    table = table[jax.random.permutation(jax.random.fold_in(own, 1), rows)]
    offset_by = jax.random.randint(jax.random.fold_in(own, 2), (rows, 1), 0, top)
    return jnp.take_along_axis(table, (jnp.arange(top)[None, :] + offset_by) % top, axis=1)


def load_shares(number_of, total, limit, skew, full):
    weights = [(1 << 20) // math.isqrt(grade ** skew) + 1 for grade in range(1, number_of + 1)]
    largest = limit if full else min(limit, max(-(-total // number_of), total * weights[0] // sum(weights)))
    least = 1 if total - largest >= number_of - 1 else 0
    counts, spare = [largest] + [least] * (number_of - 1), total - largest - least * (number_of - 1)
    while spare > 0:
        movable = [i for i in range(1, number_of) if counts[i] < largest] or [i for i in range(1, number_of) if counts[i] < limit]
        pool, budget = sum([weights[i] for i in movable]), spare
        for i in movable:
            more = min(limit - counts[i], max(1, budget * weights[i] // pool), spare)
            counts[i] = counts[i] + more
            spare = spare - more
    return np.array(counts)


def centred(stream_key, dims, width, bound, pieces=(), kind=jnp.bfloat16):
    values = width * jax.random.normal(stream_key, dims, jnp.float32)
    if pieces:
        values = values * levels(stream_key, dims, pieces, -0.22, 0.18)
    return jnp.clip(values, -bound, bound).astype(kind)


def setup_inputs(seed: int = 0) -> dict:
    splits = jax.random.split(jax.random.key(seed), 7)
    tokens = centred(splits[0], (TOKENS, D), 1.0, 6.0, ((0, 256),))
    expert_ids_keys = jax.random.split(jax.random.fold_in(splits[1], 1), TOKENS // TOK_DEV)
    expert_ids_turns = jax.random.permutation(jax.random.fold_in(splits[1], 3), TOKENS // TOK_DEV)
    expert_ids = jax.vmap(lambda own, number: shared_out(jax.random.fold_in(splits[1], 2), own, number, TOK_DEV, EXPERTS, TOP, CAP, 2))(expert_ids_keys, expert_ids_turns).reshape((TOKENS, TOP))
    gate_probs = jnp.clip(0.1 + 0.9 * jax.random.uniform(splits[2], (TOKENS, TOP), jnp.float32) ** levels(splits[2], (TOKENS, TOP), ((0, 256),), -0.2, 0.2), 0.1, 1.0)
    w_up = centred(splits[3], (D, FF_ALL), D ** -0.5, 0.09375, ((0, 4), (1, 64)))
    w_down = centred(splits[4], (FF_ALL, D), FFW ** -0.5, 0.0546875, ((0, 64), (1, 4)))
    cotangent = centred(splits[5], (TOKENS, D), 0.25, 1.5, ((0, 256),))
    return {"tokens": tokens, "expert_ids": expert_ids, "gate_probs": gate_probs, "w_up": w_up, "w_down": w_down, "cotangent": cotangent}


def silu_slope(activation):
    sigmoid_val = jax.nn.sigmoid(activation)
    return sigmoid_val * (1.0 + activation * (1.0 - sigmoid_val))


def take_group(array_in, group_index):
    shaped = array_in.reshape(N_EP, N_FSDP, CAP, array_in.shape[-1])
    return shaped[:, group_index].reshape(N_EP * CAP, array_in.shape[-1])


def reference(tokens, expert_ids, gate_probs, w_up, w_down, cotangent):
    features = tokens
    devices = TOKENS // TOK_DEV
    holder = jnp.arange(TOKENS, dtype=jnp.int32) // TOK_DEV
    cot_float = cotangent.astype(jnp.float32)
    grads_up = []
    grads_down = []
    for expert in range(2):
        matches = expert_ids == expert
        picked = jnp.any(matches, axis=1)
        weighting = jnp.sum(jnp.where(matches, gate_probs, 0.0), axis=1)
        scaled = (weighting[:, None] * cot_float).astype(jnp.bfloat16)
        counts_dev = picked.astype(jnp.int32).reshape(devices, TOK_DEV)
        slot_index = (jnp.cumsum(counts_dev, axis=1) - counts_dev).reshape(TOKENS).astype(jnp.int32)
        target = jnp.where(picked, holder * CAP + slot_index, devices * CAP).astype(jnp.int32)
        fed_rows = jnp.zeros((devices * CAP, D), jnp.bfloat16).at[target].set(features, mode="drop")
        fed_grads = jnp.zeros((devices * CAP, D), jnp.bfloat16).at[target].set(scaled, mode="drop")
        up_block = w_up[:, expert * FFW:(expert + 1) * FFW]
        down_block = w_down[expert * FFW:(expert + 1) * FFW]
        pre_act = jnp.dot(fed_rows, up_block, preferred_element_type=jnp.float32)
        hidden = jax.nn.silu(pre_act).astype(jnp.bfloat16)
        back_grad = jnp.dot(fed_grads, down_block.T, preferred_element_type=jnp.float32)
        inner_grad = (back_grad * silu_slope(pre_act)).astype(jnp.bfloat16)
        total_down = jnp.zeros((FFW, D), jnp.float32)
        total_up = jnp.zeros((D, FFW), jnp.float32)
        for group_index in range(N_FSDP):
            part_down = jnp.dot(take_group(hidden, group_index).T, take_group(fed_grads, group_index), preferred_element_type=jnp.float32).astype(jnp.bfloat16)
            part_down = lax.optimization_barrier(part_down)
            total_down = total_down + part_down.astype(jnp.float32)
            part_up = jnp.dot(take_group(fed_rows, group_index).T, take_group(inner_grad, group_index), preferred_element_type=jnp.float32).astype(jnp.bfloat16)
            part_up = lax.optimization_barrier(part_up)
            total_up = total_up + part_up.astype(jnp.float32)
        grads_down.append(total_down.astype(jnp.bfloat16))
        grads_up.append(total_up.astype(jnp.bfloat16))
    grad_up = jnp.concatenate(grads_up, axis=1)
    grad_down = jnp.concatenate(grads_down, axis=0)
    return (grad_up, grad_down)
```

```python
import functools

import jax
import jax.numpy as jnp
from jax import lax
from jax.experimental import pallas as pl
from jax.experimental.pallas import tpu as pltpu
from jax.sharding import Mesh
from jax.sharding import PartitionSpec as P

CAP = 18
AXES = ("yh", "yl", "zl", "x", "zh", "c")
F32 = jnp.float32
BF16 = jnp.bfloat16
VMEM_LIMIT = 48 * 1024 * 1024


def slots_kernel(place_ref, ids_ref, probs_ref, tok_ref, cot_ref, keep_ref, send_ref):
    tok_dev = tok_ref.shape[0]
    quarter = tok_ref.shape[1] // 4
    zh, c, yh = place_ref[0], place_ref[1], place_ref[2]
    upper = (
        lax.broadcasted_iota(jnp.int32, (tok_dev, tok_dev), 0)
        < lax.broadcasted_iota(jnp.int32, (tok_dev, tok_dev), 1)
    ).astype(BF16)
    ids = ids_ref[...]
    probs = probs_ref[...]
    place = lax.broadcasted_iota(jnp.int32, (2 * CAP, tok_dev), 0)
    tables = []
    for expert in (yh, 1 - yh):
        matches = ids == expert
        picked = jnp.any(matches, axis=0, keepdims=True)
        weight = jnp.sum(jnp.where(matches, probs, 0.0), axis=0, keepdims=True)
        flags = jnp.broadcast_to(jnp.where(picked, 1.0, 0.0), (2 * CAP, tok_dev))
        slot = jnp.dot(flags.astype(BF16), upper, preferred_element_type=F32).astype(jnp.int32)
        hot_rows = jnp.where((slot == place) & (place < CAP) & (flags > 0.5), 1.0, 0.0)
        hot_grads = jnp.where((slot == place - CAP) & (place >= CAP) & (flags > 0.5), 1.0, 0.0)
        row_weight = jnp.sum(hot_grads * weight, axis=1, keepdims=True)
        tables.append((hot_rows.astype(BF16), hot_grads.astype(BF16), row_weight))
    for half in range(2):
        for part in range(2):
            zone = (zh + half * (1 - 2 * zh)) * 2 + (c + part * (1 - 2 * c))
            lanes = pl.ds(pl.multiple_of(zone * quarter, quarter), quarter)
            tok = tok_ref[:, lanes]
            cot = cot_ref[:, lanes]
            base = (2 * half + part) * quarter
            for out, (hot_rows, hot_grads, row_weight) in zip((keep_ref, send_ref), tables, strict=True):
                rows = jnp.dot(hot_rows, tok, preferred_element_type=F32)
                grads = row_weight * jnp.dot(hot_grads, cot, preferred_element_type=F32)
                out[:, base : base + quarter] = (rows + grads).astype(BF16)


def fill_slots(place, ids, probs, tokens, cotangent):
    width = tokens.shape[1]
    vmem = pl.BlockSpec(memory_space=pltpu.VMEM)
    shape = jax.ShapeDtypeStruct((2 * CAP, width), BF16)
    return pl.pallas_call(
        slots_kernel,
        in_specs=[pl.BlockSpec(memory_space=pltpu.SMEM), vmem, vmem, vmem, vmem],
        out_specs=[vmem, vmem],
        out_shape=[shape, shape],
        compiler_params=pltpu.CompilerParams(vmem_limit_bytes=VMEM_LIMIT),
    )(place, ids, probs, tokens, cotangent)


def assemble_kernel(*refs):
    *pieces, out_ref, wide_ref, total_ref = refs
    half = out_ref.shape[1] // 2
    for k, piece in enumerate(pieces):
        wide_ref[...] = piece[...].astype(F32)
        for j in range(2):
            at = (2 * k + j) * CAP
            total_ref[at : at + CAP, :half] = wide_ref[2 * j * CAP : (2 * j + 1) * CAP, :]
            total_ref[at : at + CAP, half:] = wide_ref[(2 * j + 1) * CAP : (2 * j + 2) * CAP, :]
    out_ref[...] = total_ref[...].astype(BF16)


def assemble(*pieces):
    count, half = pieces[0].shape
    vmem = pl.BlockSpec(memory_space=pltpu.VMEM)
    rows = len(pieces) * count // 2
    return pl.pallas_call(
        assemble_kernel,
        in_specs=[vmem] * len(pieces),
        out_specs=vmem,
        out_shape=jax.ShapeDtypeStruct((rows, 2 * half), BF16),
        scratch_shapes=[pltpu.VMEM((count, half), F32), pltpu.VMEM((rows, 2 * half), F32)],
        compiler_params=pltpu.CompilerParams(vmem_limit_bytes=VMEM_LIMIT),
    )(*pieces)


def forward_kernel(*refs):
    *chunks, up_ref, down_ref, out_ref = refs
    rows, both = chunks[0].shape
    half = both // 2
    ffw = up_ref.shape[1]
    for at, ref in enumerate(chunks):
        pre = jnp.dot(ref[:, :half], up_ref[...], preferred_element_type=F32)
        back = lax.dot_general(
            ref[:, half:], down_ref[...], (((1,), (1,)), ((), ())), preferred_element_type=F32
        )
        out_ref[at * rows : (at + 1) * rows, :ffw] = pre.astype(BF16)
        out_ref[at * rows : (at + 1) * rows, ffw:] = back.astype(BF16)


def forward(up, down, *chunks):
    rows, _ = chunks[0].shape
    ffw = up.shape[1]
    vmem = pl.BlockSpec(memory_space=pltpu.VMEM)
    return pl.pallas_call(
        forward_kernel,
        in_specs=[vmem] * (len(chunks) + 2),
        out_specs=vmem,
        out_shape=jax.ShapeDtypeStruct((len(chunks) * rows, 2 * ffw), BF16),
        compiler_params=pltpu.CompilerParams(vmem_limit_bytes=VMEM_LIMIT),
    )(*chunks, up, down)


def backward_kernel(sizes, fresh, *refs):
    count = sum(sizes)
    refs = list(refs)
    sums = [(refs.pop(0), refs.pop(0)) for _ in sizes]
    chunks = [(refs.pop(0), refs.pop(0)) for _ in range(count)]
    if not fresh:
        up_in, down_in = refs.pop(0), refs.pop(0)
    up_ref, down_ref, hid_ref, inn_ref = refs
    rows = chunks[0][0].shape[0]
    half = rows // 2
    ffw = hid_ref.shape[1]

    @pl.when(pl.program_id(0) == 0)
    def _():
        at = 0
        for size, (own_ref, got_ref) in zip(sizes, sums, strict=True):
            for k in range(size):
                own = own_ref[k * rows : (k + 1) * rows, :].astype(F32)
                got = got_ref[k * rows : (k + 1) * rows, :].astype(F32)
                total = own + jnp.concatenate([got[half:], got[:half]], axis=0)
                pre = total[:, :ffw]
                back = total[:, ffw:]
                gate = 1.0 / (1.0 + jnp.exp(-pre))
                hid_ref[at : at + rows, :] = (pre * gate).astype(BF16)
                inn_ref[at : at + rows, :] = (back * (gate * (1.0 + pre * (1.0 - gate)))).astype(BF16)
                at += rows

    dims = (((0,), (0,)), ((), ()))
    grad_up = None if fresh else up_in[...]
    grad_down = None if fresh else down_in[...]
    for k, (rows_ref, grads_ref) in enumerate(chunks):
        at = k * rows
        more_up = lax.dot_general(rows_ref[...], inn_ref[at : at + rows], dims, preferred_element_type=F32)
        more_down = lax.dot_general(hid_ref[at : at + rows], grads_ref[...], dims, preferred_element_type=F32)
        grad_up = more_up if grad_up is None else grad_up + more_up
        grad_down = more_down if grad_down is None else grad_down + more_down
    up_ref[...] = grad_up.astype(up_ref.dtype)
    down_ref[...] = grad_down.astype(down_ref.dtype)


def backward(groups, totals, part=None, dtype=F32):
    first = groups[0][2][0]
    rows, both = first.shape
    half = both // 2
    ffw = groups[0][0].shape[1] // 2
    steps = 4
    tile = half // steps
    grid, base = (steps, 0) if part is None else (steps // 2, part * (steps // 2))
    sizes = tuple(len(chunks) for _, _, chunks in groups)
    fresh = totals is None
    operands, specs = [], []
    for own, got, _ in groups:
        for value in (own, got):
            operands.append(value)
            specs.append(pl.BlockSpec(value.shape, lambda i: (0, 0)))
    for _, _, chunks in groups:
        for chunk in chunks:
            operands += [chunk, chunk]
            specs.append(pl.BlockSpec((rows, tile), lambda i: (0, base + i)))
            specs.append(pl.BlockSpec((rows, tile), lambda i: (0, steps + base + i)))
    aliases = {}
    if not fresh:
        if part is None:
            aliases = {len(operands): 0, len(operands) + 1: 1}
        operands += list(totals)
        specs.append(pl.BlockSpec((tile, ffw), lambda i: (base + i, 0)))
        specs.append(pl.BlockSpec((ffw, tile), lambda i: (0, base + i)))
    kept = [pltpu.VMEM((sum(sizes) * rows, ffw), BF16)] * 2
    return pl.pallas_call(
        functools.partial(backward_kernel, sizes, fresh),
        grid=(grid,),
        in_specs=specs,
        out_specs=[
            pl.BlockSpec((tile, ffw), lambda i: (i, 0)),
            pl.BlockSpec((ffw, tile), lambda i: (0, i)),
        ],
        out_shape=[
            jax.ShapeDtypeStruct((grid * tile, ffw), dtype),
            jax.ShapeDtypeStruct((ffw, grid * tile), dtype),
        ],
        scratch_shapes=kept,
        input_output_aliases=aliases,
        compiler_params=pltpu.CompilerParams(
            vmem_limit_bytes=VMEM_LIMIT, dimension_semantics=("arbitrary",)
        ),
    )(*operands)


def ring(value, axis, by):
    count = lax.axis_size(axis)
    return lax.ppermute(value, axis, [(i, (i + by) % count) for i in range(count)])


def along_z(value, by, cross):
    count = lax.axis_size("zl")
    pairs = [
        (zl * 2 + zh, ((zl + by) % count) * 2 + (zh ^ cross)) for zl in range(count) for zh in range(2)
    ]
    return lax.ppermute(value, ("zl", "zh"), pairs)


def swap(value):
    return ring(value, "zh", 1)


def body(tokens, expert_ids, gate_probs, w_up, w_down, cotangent):
    barrier = lax.optimization_barrier
    place = jnp.stack([lax.axis_index("zh"), lax.axis_index("c"), lax.axis_index("yh")]).astype(jnp.int32)
    keep, send = fill_slots(place, expert_ids.T, gate_probs.T, tokens, cotangent)
    half = tokens.shape[1] // 2
    got = ring(send, "yh", 1)
    mine = jnp.concatenate([keep[:, :half], got[:, :half]], axis=0)
    other = jnp.concatenate([keep[:, half:], got[:, half:]], axis=0)
    mine, other = barrier((mine, other))

    s1, c0, c1 = along_z(mine, 1, 0), along_z(other, 0, 1), along_z(other, 1, 1)
    up = jnp.concatenate([w_up, ring(w_up, "c", 1)], axis=0)
    down = jnp.concatenate([w_down, ring(w_down, "c", 1)], axis=1)
    s1, c0, c1, mine, other, up, down = barrier((s1, c0, c1, mine, other, up, down))
    h1 = assemble(mine, s1, c0, c1)
    h1, mine, other = barrier((h1, mine, other))

    s2, s3, c2, c3 = along_z(mine, 2, 0), along_z(mine, 3, 0), along_z(other, 2, 1), along_z(other, 3, 1)
    h1y, h1l, h1r = ring(h1, "yl", 1), ring(h1, "x", 1), ring(h1, "x", -1)
    own0 = forward(up, down, h1)
    s2, s3, c2, c3, h1, h1y, h1l, h1r, own0 = barrier((s2, s3, c2, c3, h1, h1y, h1l, h1r, own0))
    h2 = assemble(s2, s3, c2, c3)
    h2, h1, h1y, h1l, h1r, own0 = barrier((h2, h1, h1y, h1l, h1r, own0))
    mid = h2.shape[0] // 2

    h2y, h2l, h2r = ring(h2, "yl", 1), ring(h2, "x", 1), ring(h2, "x", -1)
    got0 = swap(own0)
    own1 = forward(up, down, h1y, h1l)
    got1 = swap(own1)
    own2 = forward(up, down, h1r, h2)
    h1, h1y, h1l, h1r, h2, h2y, h2l, h2r, own0, got0, own1, got1, own2 = barrier(
        (h1, h1y, h1l, h1r, h2, h2y, h2l, h2r, own0, got0, own1, got1, own2)
    )

    h2ly, h1yl, h1yr = ring(h2l, "yl", 1), ring(h1y, "x", 1), ring(h1y, "x", -1)
    got2 = swap(own2)
    own3 = forward(up, down, h2l)
    got3 = swap(own3)
    totals = backward([(own0, got0, (h1,)), (own1, got1, (h1y, h1l))], None)
    own4 = forward(up, down, h2y, h2r)
    h1l, h1r, h2, h2y, h2l, h2r, h2ly, h1yl, h1yr, own2, got2, own3, got3, own4, totals = barrier(
        (h1l, h1r, h2, h2y, h2l, h2r, h2ly, h1yl, h1yr, own2, got2, own3, got3, own4, totals)
    )

    h2ry = ring(h2r, "yl", 1)
    h2o = jnp.concatenate([ring(h2l[:mid], "x", 1), ring(h2r[mid:], "x", -1)], axis=0)
    got4 = swap(own4)
    own5 = forward(up, down, h2ly)
    got5 = swap(own5)
    totals = backward([(own2, got2, (h1r, h2)), (own3, got3, (h2l,))], totals)
    own6 = forward(up, down, h1yl, h1yr)
    h1l, h2y, h2r, h2ly, h1yl, h1yr, h2ry, h2o, own4, got4, own5, got5, own6, totals = barrier(
        (h1l, h2y, h2r, h2ly, h1yl, h1yr, h2ry, h2o, own4, got4, own5, got5, own6, totals)
    )

    h2oy, h1o, h1yo = ring(h2o, "yl", 1), ring(h1l, "x", 1), ring(h1yr, "x", -1)
    got6 = swap(own6)
    own7 = forward(up, down, h2ry)
    got7 = swap(own7)
    totals = backward([(own4, got4, (h2y, h2r)), (own5, got5, (h2ly,))], totals)
    own8 = forward(up, down, h2o)
    h1yl, h1yr, h2ry, h2o, h2oy, h1o, h1yo, own6, got6, own7, got7, own8, totals = barrier(
        (h1yl, h1yr, h2ry, h2o, h2oy, h1o, h1yo, own6, got6, own7, got7, own8, totals)
    )

    got8 = swap(own8)
    own9 = forward(up, down, h2oy)
    got9 = swap(own9)
    own10 = forward(up, down, h1o, h1yo)
    got10 = swap(own10)
    totals = backward([(own6, got6, (h1yl, h1yr)), (own7, got7, (h2ry,))], totals)
    totals = backward([(own8, got8, (h2o,)), (own9, got9, (h2oy,))], totals)
    last = [(own10, got10, (h1o, h1yo))]
    far_up, far_down = backward(last, totals, 1, BF16)
    far_up, far_down = ring(far_up, "c", 1), ring(far_down, "c", 1)
    near_up, near_down = backward(last, totals, 0)
    return (
        (near_up + far_up.astype(F32)).astype(BF16),
        (near_down + far_down.astype(F32)).astype(BF16),
    )


def solution(mesh):
    fine = Mesh(mesh.devices.reshape(2, 2, 4, 4, 2, 2), AXES)
    ep, fsdp = AXES[:4], AXES[4:]
    rows = P(AXES, None)
    return jax.shard_map(
        body,
        mesh=fine,
        in_specs=(rows, rows, rows, P(fsdp, ep), P(ep, fsdp), rows),
        out_specs=(P(fsdp, ep), P(ep, fsdp)),
        check_vma=False,
    )
```

```python
import functools

import jax
import jax.numpy as jnp
from jax import lax
from jax.experimental import pallas as pl
from jax.experimental.pallas import tpu as pltpu
from jax.sharding import Mesh
from jax.sharding import PartitionSpec as P

CAP = 18
AXES = ("yh", "yl", "zl", "x", "zh", "c")
F32 = jnp.float32
BF16 = jnp.bfloat16
VMEM_LIMIT = 48 * 1024 * 1024


def slots_kernel(place_ref, *refs):
    sources, (keep_ref, send_ref), held, sems = refs[:4], refs[4:6], refs[6:10], refs[10:]
    copies = [
        pltpu.make_async_copy(src, dst, sem) for src, dst, sem in zip(sources, held, sems, strict=True)
    ]
    for copy in copies:
        copy.start()
    for copy in copies:
        copy.wait()
    ids_ref, probs_ref, tok_ref, cot_ref = held
    tok_dev = tok_ref.shape[0]
    quarter = tok_ref.shape[1] // 4
    zh, c, yh = place_ref[0], place_ref[1], place_ref[2]
    upper = (
        lax.broadcasted_iota(jnp.int32, (tok_dev, tok_dev), 0)
        < lax.broadcasted_iota(jnp.int32, (tok_dev, tok_dev), 1)
    ).astype(BF16)
    ids = ids_ref[...]
    probs = probs_ref[...]
    place = lax.broadcasted_iota(jnp.int32, (2 * CAP, tok_dev), 0)
    tables = []
    for expert in (yh, 1 - yh):
        matches = ids == expert
        picked = jnp.any(matches, axis=0, keepdims=True)
        weight = jnp.sum(jnp.where(matches, probs, 0.0), axis=0, keepdims=True)
        flags = jnp.broadcast_to(jnp.where(picked, 1.0, 0.0), (2 * CAP, tok_dev))
        slot = jnp.dot(flags.astype(BF16), upper, preferred_element_type=F32).astype(jnp.int32)
        hot_rows = jnp.where((slot == place) & (place < CAP) & (flags > 0.5), 1.0, 0.0)
        hot_grads = jnp.where((slot == place - CAP) & (place >= CAP) & (flags > 0.5), 1.0, 0.0)
        row_weight = jnp.sum(hot_grads * weight, axis=1, keepdims=True)
        tables.append((hot_rows.astype(BF16), hot_grads.astype(BF16), row_weight))
    for half in range(2):
        for part in range(2):
            zone = (zh + half * (1 - 2 * zh)) * 2 + (c + part * (1 - 2 * c))
            lanes = pl.ds(pl.multiple_of(zone * quarter, quarter), quarter)
            tok = tok_ref[:, lanes]
            cot = cot_ref[:, lanes]
            base = (2 * half + part) * quarter
            for out, (hot_rows, hot_grads, row_weight) in zip((keep_ref, send_ref), tables, strict=True):
                rows = jnp.dot(hot_rows, tok, preferred_element_type=F32)
                grads = row_weight * jnp.dot(hot_grads, cot, preferred_element_type=F32)
                out[:, base : base + quarter] = (rows + grads).astype(BF16)


def fill_slots(place, ids, probs, tokens, cotangent):
    width = tokens.shape[1]
    vmem = pl.BlockSpec(memory_space=pltpu.VMEM)
    shape = jax.ShapeDtypeStruct((2 * CAP, width), BF16)
    return pl.pallas_call(
        slots_kernel,
        in_specs=[pl.BlockSpec(memory_space=pltpu.SMEM)] + [pl.BlockSpec(memory_space=pltpu.HBM)] * 4,
        out_specs=[vmem, vmem],
        out_shape=[shape, shape],
        scratch_shapes=[pltpu.VMEM(v.shape, v.dtype) for v in (ids, probs, tokens, cotangent)]
        + [pltpu.SemaphoreType.DMA] * 4,
        compiler_params=pltpu.CompilerParams(vmem_limit_bytes=VMEM_LIMIT),
    )(place, ids, probs, tokens, cotangent)


def assemble_kernel(*refs):
    *pieces, out_ref, wide_ref, total_ref = refs
    half = out_ref.shape[1] // 2
    at = 0
    for piece in pieces:
        count = piece.shape[0]
        wide_ref[:count, :] = piece[...].astype(F32)
        for j in range(0, count, 2 * CAP):
            total_ref[at : at + CAP, :half] = wide_ref[j : j + CAP, :]
            total_ref[at : at + CAP, half:] = wide_ref[j + CAP : j + 2 * CAP, :]
            at += CAP
    out_ref[...] = total_ref[...].astype(BF16)


def assemble(*pieces):
    half = pieces[0].shape[1]
    vmem = pl.BlockSpec(memory_space=pltpu.VMEM)
    rows = sum(piece.shape[0] for piece in pieces) // 2
    most = max(piece.shape[0] for piece in pieces)
    return pl.pallas_call(
        assemble_kernel,
        in_specs=[vmem] * len(pieces),
        out_specs=vmem,
        out_shape=jax.ShapeDtypeStruct((rows, 2 * half), BF16),
        scratch_shapes=[pltpu.VMEM((most, half), F32), pltpu.VMEM((rows, 2 * half), F32)],
        compiler_params=pltpu.CompilerParams(vmem_limit_bytes=VMEM_LIMIT),
    )(*pieces)


def forward_kernel(*refs):
    *chunks, up_ref, down_ref, out_ref = refs
    rows, both = chunks[0].shape
    half = both // 2
    ffw = up_ref.shape[1]
    for at, ref in enumerate(chunks):
        pre = jnp.dot(ref[:, :half], up_ref[...], preferred_element_type=F32)
        back = lax.dot_general(
            ref[:, half:], down_ref[...], (((1,), (1,)), ((), ())), preferred_element_type=F32
        )
        out_ref[at * rows : (at + 1) * rows, :ffw] = pre.astype(BF16)
        out_ref[at * rows : (at + 1) * rows, ffw:] = back.astype(BF16)


def forward(up, down, *chunks):
    rows, _ = chunks[0].shape
    ffw = up.shape[1]
    vmem = pl.BlockSpec(memory_space=pltpu.VMEM)
    return pl.pallas_call(
        forward_kernel,
        in_specs=[vmem] * (len(chunks) + 2),
        out_specs=vmem,
        out_shape=jax.ShapeDtypeStruct((len(chunks) * rows, 2 * ffw), BF16),
        compiler_params=pltpu.CompilerParams(vmem_limit_bytes=VMEM_LIMIT),
    )(*chunks, up, down)


def backward_kernel(sizes, fresh, *refs):
    count = sum(sizes)
    refs = list(refs)
    sums = [(refs.pop(0), refs.pop(0)) for _ in sizes]
    chunks = [(refs.pop(0), refs.pop(0)) for _ in range(count)]
    if not fresh:
        up_in, down_in = refs.pop(0), refs.pop(0)
    up_ref, down_ref, hid_ref, inn_ref = refs
    rows = chunks[0][0].shape[0]
    half = rows // 2
    ffw = hid_ref.shape[1]

    @pl.when(pl.program_id(0) == 0)
    def _():
        at = 0
        for size, (own_ref, got_ref) in zip(sizes, sums, strict=True):
            for k in range(size):
                own = own_ref[k * rows : (k + 1) * rows, :].astype(F32)
                got = got_ref[k * rows : (k + 1) * rows, :].astype(F32)
                total = own + jnp.concatenate([got[half:], got[:half]], axis=0)
                pre = total[:, :ffw]
                back = total[:, ffw:]
                gate = 1.0 / (1.0 + jnp.exp(-pre))
                hid_ref[at : at + rows, :] = (pre * gate).astype(BF16)
                inn_ref[at : at + rows, :] = (back * (gate * (1.0 + pre * (1.0 - gate)))).astype(BF16)
                at += rows

    dims = (((0,), (0,)), ((), ()))
    grad_up = None if fresh else up_in[...]
    grad_down = None if fresh else down_in[...]
    for k, (rows_ref, grads_ref) in enumerate(chunks):
        at = k * rows
        more_up = lax.dot_general(rows_ref[...], inn_ref[at : at + rows], dims, preferred_element_type=F32)
        more_down = lax.dot_general(hid_ref[at : at + rows], grads_ref[...], dims, preferred_element_type=F32)
        grad_up = more_up if grad_up is None else grad_up + more_up
        grad_down = more_down if grad_down is None else grad_down + more_down
    up_ref[...] = grad_up.astype(up_ref.dtype)
    down_ref[...] = grad_down.astype(down_ref.dtype)


def backward(groups, totals, part=None, dtype=F32):
    first = groups[0][2][0]
    rows, both = first.shape
    half = both // 2
    ffw = groups[0][0].shape[1] // 2
    steps = 4
    tile = half // steps
    grid, base = (steps, 0) if part is None else (steps // 2, part * (steps // 2))
    sizes = tuple(len(chunks) for _, _, chunks in groups)
    fresh = totals is None
    operands, specs = [], []
    for own, got, _ in groups:
        for value in (own, got):
            operands.append(value)
            specs.append(pl.BlockSpec(value.shape, lambda i: (0, 0)))
    for _, _, chunks in groups:
        for chunk in chunks:
            operands += [chunk, chunk]
            specs.append(pl.BlockSpec((rows, tile), lambda i: (0, base + i)))
            specs.append(pl.BlockSpec((rows, tile), lambda i: (0, steps + base + i)))
    aliases = {}
    if not fresh:
        if part is None:
            aliases = {len(operands): 0, len(operands) + 1: 1}
        operands += list(totals)
        specs.append(pl.BlockSpec((tile, ffw), lambda i: (base + i, 0)))
        specs.append(pl.BlockSpec((ffw, tile), lambda i: (0, base + i)))
    kept = [pltpu.VMEM((sum(sizes) * rows, ffw), BF16)] * 2
    return pl.pallas_call(
        functools.partial(backward_kernel, sizes, fresh),
        grid=(grid,),
        in_specs=specs,
        out_specs=[
            pl.BlockSpec((tile, ffw), lambda i: (i, 0)),
            pl.BlockSpec((ffw, tile), lambda i: (0, i)),
        ],
        out_shape=[
            jax.ShapeDtypeStruct((grid * tile, ffw), dtype),
            jax.ShapeDtypeStruct((ffw, grid * tile), dtype),
        ],
        scratch_shapes=kept,
        input_output_aliases=aliases,
        compiler_params=pltpu.CompilerParams(
            vmem_limit_bytes=VMEM_LIMIT, dimension_semantics=("arbitrary",)
        ),
    )(*operands)


def ring(value, axis, by):
    count = lax.axis_size(axis)
    return lax.ppermute(value, axis, [(i, (i + by) % count) for i in range(count)])


def along_z(value, by, cross):
    count = lax.axis_size("zl")
    pairs = [
        (zl * 2 + zh, ((zl + by) % count) * 2 + (zh ^ cross)) for zl in range(count) for zh in range(2)
    ]
    return lax.ppermute(value, ("zl", "zh"), pairs)


def swap(value):
    return ring(value, "zh", 1)


def body(tokens, expert_ids, gate_probs, w_up, w_down, cotangent):
    barrier = lax.optimization_barrier
    place = jnp.stack([lax.axis_index("zh"), lax.axis_index("c"), lax.axis_index("yh")]).astype(jnp.int32)
    keep, send = fill_slots(place, expert_ids.T, gate_probs.T, tokens, cotangent)
    half = tokens.shape[1] // 2
    k_mine, k_other = keep[:, :half], keep[:, half:]

    got = ring(send, "yh", 1)
    ks2, kc0, kc2 = along_z(k_mine, 2, 0), along_z(k_other, 0, 1), along_z(k_other, 2, 1)
    g_mine, g_other = got[:, :half], got[:, half:]
    gs2, gc0, gc2 = along_z(g_mine, 2, 0), along_z(g_other, 0, 1), along_z(g_other, 2, 1)
    mine = jnp.concatenate([k_mine, g_mine], axis=0)
    other = jnp.concatenate([k_other, g_other], axis=0)
    up = jnp.concatenate([w_up, ring(w_up, "c", 1)], axis=0)
    down = jnp.concatenate([w_down, ring(w_down, "c", 1)], axis=1)
    ks2, kc0, kc2, gs2, gc0, gc2, mine, other, up, down = barrier(
        (ks2, kc0, kc2, gs2, gc0, gc2, mine, other, up, down)
    )
    h1 = assemble(mine, ks2, gs2, kc0, gc0, kc2, gc2)
    h1, mine, other = barrier((h1, mine, other))

    s1, s3, c1, c3 = along_z(mine, 1, 0), along_z(mine, 3, 0), along_z(other, 1, 1), along_z(other, 3, 1)
    h1y, h1l, h1r = ring(h1, "yl", 1), ring(h1, "x", 1), ring(h1, "x", -1)
    own0 = forward(up, down, h1)
    s1, s3, c1, c3, h1, h1y, h1l, h1r, own0 = barrier((s1, s3, c1, c3, h1, h1y, h1l, h1r, own0))
    h2 = assemble(s1, s3, c1, c3)
    h2, h1, h1y, h1l, h1r, own0 = barrier((h2, h1, h1y, h1l, h1r, own0))
    mid = h2.shape[0] // 2

    h2y, h2l, h2r = ring(h2, "yl", 1), ring(h2, "x", 1), ring(h2, "x", -1)
    got0 = swap(own0)
    own1 = forward(up, down, h1y, h1l)
    got1 = swap(own1)
    own2 = forward(up, down, h1r, h2)
    h1, h1y, h1l, h1r, h2, h2y, h2l, h2r, own0, got0, own1, got1, own2 = barrier(
        (h1, h1y, h1l, h1r, h2, h2y, h2l, h2r, own0, got0, own1, got1, own2)
    )

    h2ly, h1yl, h1yr = ring(h2l, "yl", 1), ring(h1y, "x", 1), ring(h1y, "x", -1)
    got2 = swap(own2)
    own3 = forward(up, down, h2l)
    got3 = swap(own3)
    totals = backward([(own0, got0, (h1,)), (own1, got1, (h1y, h1l))], None)
    own4 = forward(up, down, h2y, h2r)
    h1l, h1r, h2, h2y, h2l, h2r, h2ly, h1yl, h1yr, own2, got2, own3, got3, own4, totals = barrier(
        (h1l, h1r, h2, h2y, h2l, h2r, h2ly, h1yl, h1yr, own2, got2, own3, got3, own4, totals)
    )

    h2ry = ring(h2r, "yl", 1)
    h2o = jnp.concatenate([ring(h2l[:mid], "x", 1), ring(h2r[mid:], "x", -1)], axis=0)
    got4 = swap(own4)
    own5 = forward(up, down, h2ly)
    got5 = swap(own5)
    totals = backward([(own2, got2, (h1r, h2)), (own3, got3, (h2l,))], totals)
    own6 = forward(up, down, h1yl, h1yr)
    h1l, h2y, h2r, h2ly, h1yl, h1yr, h2ry, h2o, own4, got4, own5, got5, own6, totals = barrier(
        (h1l, h2y, h2r, h2ly, h1yl, h1yr, h2ry, h2o, own4, got4, own5, got5, own6, totals)
    )

    h2oy, h1o, h1yo = ring(h2o, "yl", 1), ring(h1l, "x", 1), ring(h1yr, "x", -1)
    got6 = swap(own6)
    own7 = forward(up, down, h2ry)
    got7 = swap(own7)
    totals = backward([(own4, got4, (h2y, h2r)), (own5, got5, (h2ly,))], totals)
    own8 = forward(up, down, h2o)
    h1yl, h1yr, h2ry, h2o, h2oy, h1o, h1yo, own6, got6, own7, got7, own8, totals = barrier(
        (h1yl, h1yr, h2ry, h2o, h2oy, h1o, h1yo, own6, got6, own7, got7, own8, totals)
    )

    got8 = swap(own8)
    own9 = forward(up, down, h2oy)
    got9 = swap(own9)
    own10 = forward(up, down, h1o, h1yo)
    got10 = swap(own10)
    totals = backward([(own6, got6, (h1yl, h1yr)), (own7, got7, (h2ry,))], totals)
    last = [(own8, got8, (h2o,)), (own9, got9, (h2oy,)), (own10, got10, (h1o, h1yo))]
    far_up, far_down = backward(last, totals, 1, BF16)
    far_up, far_down = ring(far_up, "c", 1), ring(far_down, "c", 1)
    near_up, near_down = backward(last, totals, 0)
    return (
        (near_up + far_up.astype(F32)).astype(BF16),
        (near_down + far_down.astype(F32)).astype(BF16),
    )


def solution(mesh):
    fine = Mesh(mesh.devices.reshape(2, 2, 4, 4, 2, 2), AXES)
    ep, fsdp = AXES[:4], AXES[4:]
    rows = P(AXES, None)
    return jax.shard_map(
        body,
        mesh=fine,
        in_specs=(rows, rows, rows, P(fsdp, ep), P(ep, fsdp), rows),
        out_specs=(P(fsdp, ep), P(ep, fsdp)),
        check_vma=False,
    )
```

```python
import functools

import jax
import jax.numpy as jnp
from jax import lax
from jax.experimental import pallas as pl
from jax.experimental.pallas import tpu as pltpu
from jax.sharding import Mesh
from jax.sharding import PartitionSpec as P

CAP = 18
AXES = ("yh", "yl", "zl", "x", "zh", "c")
F32 = jnp.float32
BF16 = jnp.bfloat16
VMEM_LIMIT = 32 * 1024 * 1024


def slots_kernel(place_ref, *refs):
    sources, (keep_ref, send_ref), held, sems = refs[:4], refs[4:6], refs[6:10], refs[10:]
    copies = [
        pltpu.make_async_copy(src, dst, sem) for src, dst, sem in zip(sources, held, sems, strict=True)
    ]
    for copy in copies:
        copy.start()
    for copy in copies:
        copy.wait()
    ids_ref, probs_ref, tok_ref, cot_ref = held
    tok_dev = tok_ref.shape[0]
    quarter = tok_ref.shape[1] // 4
    zh, c, yh = place_ref[0], place_ref[1], place_ref[2]
    upper = (
        lax.broadcasted_iota(jnp.int32, (tok_dev, tok_dev), 0)
        < lax.broadcasted_iota(jnp.int32, (tok_dev, tok_dev), 1)
    ).astype(BF16)
    ids = ids_ref[...]
    probs = probs_ref[...]
    place = lax.broadcasted_iota(jnp.int32, (2 * CAP, tok_dev), 0)
    tables = []
    for expert in (yh, 1 - yh):
        matches = ids == expert
        picked = jnp.any(matches, axis=0, keepdims=True)
        weight = jnp.sum(jnp.where(matches, probs, 0.0), axis=0, keepdims=True)
        flags = jnp.broadcast_to(jnp.where(picked, 1.0, 0.0), (2 * CAP, tok_dev))
        slot = jnp.dot(flags.astype(BF16), upper, preferred_element_type=F32).astype(jnp.int32)
        hot_rows = jnp.where((slot == place) & (place < CAP) & (flags > 0.5), 1.0, 0.0)
        hot_grads = jnp.where((slot == place - CAP) & (place >= CAP) & (flags > 0.5), 1.0, 0.0)
        row_weight = jnp.sum(hot_grads * weight, axis=1, keepdims=True)
        tables.append((hot_rows.astype(BF16), hot_grads.astype(BF16), row_weight))
    for half in range(2):
        for part in range(2):
            zone = (zh + half * (1 - 2 * zh)) * 2 + (c + part * (1 - 2 * c))
            lanes = pl.ds(pl.multiple_of(zone * quarter, quarter), quarter)
            tok = tok_ref[:, lanes]
            cot = cot_ref[:, lanes]
            base = (2 * half + part) * quarter
            for out, (hot_rows, hot_grads, row_weight) in zip((keep_ref, send_ref), tables, strict=True):
                rows = jnp.dot(hot_rows, tok, preferred_element_type=F32)
                grads = row_weight * jnp.dot(hot_grads, cot, preferred_element_type=F32)
                out[:, base : base + quarter] = (rows + grads).astype(BF16)


def fill_slots(place, ids, probs, tokens, cotangent):
    width = tokens.shape[1]
    vmem = pl.BlockSpec(memory_space=pltpu.VMEM)
    shape = jax.ShapeDtypeStruct((2 * CAP, width), BF16)
    return pl.pallas_call(
        slots_kernel,
        in_specs=[pl.BlockSpec(memory_space=pltpu.SMEM)] + [pl.BlockSpec(memory_space=pltpu.HBM)] * 4,
        out_specs=[vmem, vmem],
        out_shape=[shape, shape],
        scratch_shapes=[pltpu.VMEM(v.shape, v.dtype) for v in (ids, probs, tokens, cotangent)]
        + [pltpu.SemaphoreType.DMA] * 4,
        compiler_params=pltpu.CompilerParams(vmem_limit_bytes=VMEM_LIMIT),
    )(place, ids, probs, tokens, cotangent)


def assemble_kernel(*refs):
    *pieces, out_ref, wide_ref, total_ref = refs
    half = out_ref.shape[1] // 2
    at = 0
    for piece in pieces:
        count = piece.shape[0]
        wide_ref[:count, :] = piece[...].astype(F32)
        for j in range(0, count, 2 * CAP):
            total_ref[at : at + CAP, :half] = wide_ref[j : j + CAP, :]
            total_ref[at : at + CAP, half:] = wide_ref[j + CAP : j + 2 * CAP, :]
            at += CAP
    out_ref[...] = total_ref[...].astype(BF16)


def assemble(*pieces):
    half = pieces[0].shape[1]
    vmem = pl.BlockSpec(memory_space=pltpu.VMEM)
    rows = sum(piece.shape[0] for piece in pieces) // 2
    most = max(piece.shape[0] for piece in pieces)
    return pl.pallas_call(
        assemble_kernel,
        in_specs=[vmem] * len(pieces),
        out_specs=vmem,
        out_shape=jax.ShapeDtypeStruct((rows, 2 * half), BF16),
        scratch_shapes=[pltpu.VMEM((most, half), F32), pltpu.VMEM((rows, 2 * half), F32)],
        compiler_params=pltpu.CompilerParams(vmem_limit_bytes=VMEM_LIMIT),
    )(*pieces)


def forward_kernel(*refs):
    *chunks, up_ref, down_ref, out_ref = refs
    rows, both = chunks[0].shape
    half = both // 2
    ffw = up_ref.shape[1]
    for at, ref in enumerate(chunks):
        pre = jnp.dot(ref[:, :half], up_ref[...], preferred_element_type=F32)
        back = lax.dot_general(
            ref[:, half:], down_ref[...], (((1,), (1,)), ((), ())), preferred_element_type=F32
        )
        out_ref[at * rows : (at + 1) * rows, :ffw] = pre.astype(BF16)
        out_ref[at * rows : (at + 1) * rows, ffw:] = back.astype(BF16)


def forward(up, down, *chunks):
    rows, _ = chunks[0].shape
    ffw = up.shape[1]
    vmem = pl.BlockSpec(memory_space=pltpu.VMEM)
    return pl.pallas_call(
        forward_kernel,
        in_specs=[vmem] * (len(chunks) + 2),
        out_specs=vmem,
        out_shape=jax.ShapeDtypeStruct((len(chunks) * rows, 2 * ffw), BF16),
        compiler_params=pltpu.CompilerParams(vmem_limit_bytes=VMEM_LIMIT),
    )(*chunks, up, down)


TRANSPOSED = (((0,), (0,)), ((), ()))


def finish_hidden(sizes, sums, rows, hid_ref, inn_ref):
    half = rows // 2
    at = 0
    for size, (own_ref, got_ref) in zip(sizes, sums, strict=True):
        ffw = own_ref.shape[1] // 2
        for k in range(size):
            place = slice(k * rows, (k + 1) * rows)

            def total(lanes, own_ref=own_ref, got_ref=got_ref, place=place):
                got = got_ref[place, lanes].astype(F32)
                return own_ref[place, lanes].astype(F32) + jnp.concatenate([got[half:], got[:half]], axis=0)

            pre = total(slice(0, ffw))
            gate = 1.0 / (1.0 + jnp.exp(-pre))
            if hid_ref is not None:
                hid_ref[at : at + rows, :] = (pre * gate).astype(BF16)
            if inn_ref is not None:
                back = total(slice(ffw, 2 * ffw))
                inn_ref[at : at + rows, :] = (back * (gate * (1.0 + pre * (1.0 - gate)))).astype(BF16)
            at += rows


def backward_kernel(sizes, fresh, tile, *refs):
    refs = list(refs)
    sums = [(refs.pop(0), refs.pop(0)) for _ in sizes]
    chunks = [refs.pop(0) for _ in range(sum(sizes))]
    if not fresh:
        up_in, down_in = refs.pop(0), refs.pop(0)
    up_ref, down_ref, hid_ref, inn_ref = refs
    rows, both = chunks[0].shape
    half = both // 2
    finish_hidden(sizes, sums, rows, hid_ref, inn_ref)
    for lane in range(0, half, tile):
        grad_up = None if fresh else up_in[lane : lane + tile, :]
        grad_down = None if fresh else down_in[:, lane : lane + tile]
        for k, chunk in enumerate(chunks):
            at = slice(k * rows, (k + 1) * rows)
            more_up = lax.dot_general(
                chunk[:, lane : lane + tile], inn_ref[at], TRANSPOSED, preferred_element_type=F32
            )
            more_down = lax.dot_general(
                hid_ref[at], chunk[:, half + lane : half + lane + tile], TRANSPOSED, preferred_element_type=F32
            )
            grad_up = more_up if grad_up is None else grad_up + more_up
            grad_down = more_down if grad_down is None else grad_down + more_down
        up_ref[lane : lane + tile, :] = grad_up
        down_ref[:, lane : lane + tile] = grad_down


def backward(groups, totals):
    rows, both = groups[0][2][0].shape
    half = both // 2
    ffw = groups[0][0].shape[1] // 2
    sizes = tuple(len(chunks) for _, _, chunks in groups)
    fresh = totals is None
    operands = [value for own, got, _ in groups for value in (own, got)]
    operands += [chunk for _, _, chunks in groups for chunk in chunks]
    aliases = {} if fresh else {len(operands): 0, len(operands) + 1: 1}
    operands += [] if fresh else list(totals)
    vmem = pl.BlockSpec(memory_space=pltpu.VMEM)
    return pl.pallas_call(
        functools.partial(backward_kernel, sizes, fresh, half // 4),
        in_specs=[vmem] * len(operands),
        out_specs=[vmem, vmem],
        out_shape=[jax.ShapeDtypeStruct((half, ffw), F32), jax.ShapeDtypeStruct((ffw, half), F32)],
        scratch_shapes=[pltpu.VMEM((sum(sizes) * rows, ffw), BF16)] * 2,
        input_output_aliases=aliases,
        compiler_params=pltpu.CompilerParams(vmem_limit_bytes=VMEM_LIMIT),
    )(*operands)


def last_kernel(sizes, is_up, part, tile, added, *refs):
    refs = list(refs)
    sums = [(refs.pop(0), refs.pop(0)) for _ in sizes]
    chunks = [refs.pop(0) for _ in range(sum(sizes))]
    total_ref = refs.pop(0)
    add_ref = refs.pop(0) if added else None
    out_ref, mid_ref = refs
    rows, both = chunks[0].shape
    half = both // 2
    if is_up:
        finish_hidden(sizes, sums, rows, None, mid_ref)
    else:
        finish_hidden(sizes, sums, rows, mid_ref, None)
    for lane in range(0, half // 2, tile):
        source = part * (half // 2) + lane
        near = slice(lane, lane + tile)
        if is_up:
            grad = total_ref[source : source + tile, :]
        else:
            grad = total_ref[:, source : source + tile]
        for k, chunk in enumerate(chunks):
            at = slice(k * rows, (k + 1) * rows)
            if is_up:
                grad += lax.dot_general(
                    chunk[:, source : source + tile], mid_ref[at], TRANSPOSED, preferred_element_type=F32
                )
            else:
                lanes = slice(half + source, half + source + tile)
                grad += lax.dot_general(mid_ref[at], chunk[:, lanes], TRANSPOSED, preferred_element_type=F32)
        if is_up:
            grad = grad if add_ref is None else grad + add_ref[near, :].astype(F32)
            out_ref[near, :] = grad.astype(BF16)
        else:
            grad = grad if add_ref is None else grad + add_ref[:, near].astype(F32)
            out_ref[:, near] = grad.astype(BF16)


def last(groups, total, is_up, part, added=None):
    rows, both = groups[0][2][0].shape
    half = both // 2
    ffw = groups[0][0].shape[1] // 2
    sizes = tuple(len(chunks) for _, _, chunks in groups)
    operands = [value for own, got, _ in groups for value in (own, got)]
    operands += [chunk for _, _, chunks in groups for chunk in chunks]
    operands.append(total)
    if added is not None:
        operands.append(added)
    vmem = pl.BlockSpec(memory_space=pltpu.VMEM)
    shape = (half // 2, ffw) if is_up else (ffw, half // 2)
    return pl.pallas_call(
        functools.partial(last_kernel, sizes, is_up, part, half // 4, added is not None),
        in_specs=[vmem] * len(operands),
        out_specs=vmem,
        out_shape=jax.ShapeDtypeStruct(shape, BF16),
        scratch_shapes=[pltpu.VMEM((sum(sizes) * rows, ffw), BF16)],
        compiler_params=pltpu.CompilerParams(vmem_limit_bytes=VMEM_LIMIT),
    )(*operands)


def ring(value, axis, by):
    count = lax.axis_size(axis)
    return lax.ppermute(value, axis, [(i, (i + by) % count) for i in range(count)])


def along_z(value, by, cross, over=0):
    count = lax.axis_size("zl")

    def at(yh, zl, zh):
        return (yh * count + zl) * 2 + zh

    pairs = [
        (at(yh, zl, zh), at(yh ^ over, (zl + by) % count, zh ^ cross))
        for yh in range(2)
        for zl in range(count)
        for zh in range(2)
    ]
    return lax.ppermute(value, ("yh", "zl", "zh"), pairs)


def swap(value):
    return ring(value, "zh", 1)


def body(tokens, expert_ids, gate_probs, w_up, w_down, cotangent):
    barrier = lax.optimization_barrier
    place = jnp.stack([lax.axis_index("zh"), lax.axis_index("c"), lax.axis_index("yh")]).astype(jnp.int32)
    keep, send = fill_slots(place, expert_ids.T, gate_probs.T, tokens, cotangent)
    half = tokens.shape[1] // 2
    k_mine, k_other = keep[:, :half], keep[:, half:]

    got = ring(send, "yh", 1)
    ks2, kc0, kc2 = along_z(k_mine, 2, 0), along_z(k_other, 0, 1), along_z(k_other, 2, 1)
    g_mine, g_other = got[:, :half], got[:, half:]
    s_mine, s_other = send[:, :half], send[:, half:]
    gs2, gc0, gc2 = along_z(s_mine, 2, 0, 1), along_z(s_other, 0, 1, 1), along_z(s_other, 2, 1, 1)
    mine = jnp.concatenate([k_mine, g_mine], axis=0)
    other = jnp.concatenate([k_other, g_other], axis=0)
    up = jnp.concatenate([w_up, ring(w_up, "c", 1)], axis=0)
    down = jnp.concatenate([w_down, ring(w_down, "c", 1)], axis=1)
    ks2, kc0, kc2, gs2, gc0, gc2, mine, other, up, down = barrier(
        (ks2, kc0, kc2, gs2, gc0, gc2, mine, other, up, down)
    )
    h1 = assemble(mine, ks2, gs2, kc0, gc0, kc2, gc2)
    h1, mine, other = barrier((h1, mine, other))

    s1, s3, c1, c3 = along_z(mine, 1, 0), along_z(mine, 3, 0), along_z(other, 1, 1), along_z(other, 3, 1)
    h1y, h1l, h1r = ring(h1, "yl", 1), ring(h1, "x", 1), ring(h1, "x", -1)
    own0 = forward(up, down, h1)
    s1, s3, c1, c3, h1, h1y, h1l, h1r, own0 = barrier((s1, s3, c1, c3, h1, h1y, h1l, h1r, own0))
    h2 = assemble(s1, s3, c1, c3)
    h2, h1, h1y, h1l, h1r, own0 = barrier((h2, h1, h1y, h1l, h1r, own0))
    mid = h2.shape[0] // 2

    h2y, h2l, h2r = ring(h2, "yl", 1), ring(h2, "x", 1), ring(h2, "x", -1)
    got0 = swap(own0)
    own1 = forward(up, down, h1y, h1l)
    got1 = swap(own1)
    own2 = forward(up, down, h1r, h2)
    h1, h1y, h1l, h1r, h2, h2y, h2l, h2r, own0, got0, own1, got1, own2 = barrier(
        (h1, h1y, h1l, h1r, h2, h2y, h2l, h2r, own0, got0, own1, got1, own2)
    )

    h2ly, h1yl, h1yr = ring(h2l, "yl", 1), ring(h1y, "x", 1), ring(h1y, "x", -1)
    got2 = swap(own2)
    own3 = forward(up, down, h2l)
    got3 = swap(own3)
    totals = backward([(own0, got0, (h1,)), (own1, got1, (h1y, h1l))], None)
    own4 = forward(up, down, h2y, h2r)
    h1l, h1r, h2, h2y, h2l, h2r, h2ly, h1yl, h1yr, own2, got2, own3, got3, own4, totals = barrier(
        (h1l, h1r, h2, h2y, h2l, h2r, h2ly, h1yl, h1yr, own2, got2, own3, got3, own4, totals)
    )

    h2ry = ring(h2r, "yl", 1)
    h2o = jnp.concatenate([ring(h2l[:mid], "x", 1), ring(h2r[mid:], "x", -1)], axis=0)
    got4 = swap(own4)
    own5 = forward(up, down, h2ly)
    got5 = swap(own5)
    totals = backward([(own2, got2, (h1r, h2)), (own3, got3, (h2l,))], totals)
    own6 = forward(up, down, h1yl, h1yr)
    h1l, h2y, h2r, h2ly, h1yl, h1yr, h2ry, h2o, own4, got4, own5, got5, own6, totals = barrier(
        (h1l, h2y, h2r, h2ly, h1yl, h1yr, h2ry, h2o, own4, got4, own5, got5, own6, totals)
    )

    h2oy, h1o, h1yo = ring(h2o, "yl", 1), ring(h1l, "x", 1), ring(h1yr, "x", -1)
    got6 = swap(own6)
    own7 = forward(up, down, h2ry)
    got7 = swap(own7)
    totals = backward([(own4, got4, (h2y, h2r)), (own5, got5, (h2ly,))], totals)
    own8 = forward(up, down, h2o)
    h1yl, h1yr, h2ry, h2o, h2oy, h1o, h1yo, own6, got6, own7, got7, own8, totals = barrier(
        (h1yl, h1yr, h2ry, h2o, h2oy, h1o, h1yo, own6, got6, own7, got7, own8, totals)
    )

    got8 = swap(own8)
    own9 = forward(up, down, h2oy)
    got9 = swap(own9)
    own10 = forward(up, down, h1o, h1yo)
    got10 = swap(own10)
    totals = backward([(own6, got6, (h1yl, h1yr)), (own7, got7, (h2ry,))], totals)
    groups = [(own8, got8, (h2o,)), (own9, got9, (h2oy,)), (own10, got10, (h1o, h1yo))]
    far_up = ring(last(groups, totals[0], True, 1), "c", 1)
    far_down = ring(last(groups, totals[1], False, 1), "c", 1)
    return last(groups, totals[0], True, 0, far_up), last(groups, totals[1], False, 0, far_down)


def solution(mesh):
    fine = Mesh(mesh.devices.reshape(2, 2, 4, 4, 2, 2), AXES)
    ep, fsdp = AXES[:4], AXES[4:]
    rows = P(AXES, None)
    return jax.shard_map(
        body,
        mesh=fine,
        in_specs=(rows, rows, rows, P(fsdp, ep), P(ep, fsdp), rows),
        out_specs=(P(fsdp, ep), P(ep, fsdp)),
        check_vma=False,
    )
```

```python
import functools

import jax
import jax.numpy as jnp
from jax import lax
from jax.experimental import pallas as pl
from jax.experimental.pallas import tpu as pltpu
from jax.sharding import Mesh
from jax.sharding import PartitionSpec as P

CAP = 18
AXES = ("yh", "yl", "zl", "x", "zh", "c")
F32 = jnp.float32
BF16 = jnp.bfloat16
VMEM_LIMIT = 32 * 1024 * 1024


def slots_kernel(place_ref, *refs):
    sources, (keep_ref, send_ref), held, sems = refs[:4], refs[4:6], refs[6:10], refs[10:]
    copies = [
        pltpu.make_async_copy(src, dst, sem) for src, dst, sem in zip(sources, held, sems, strict=True)
    ]
    for copy in copies:
        copy.start()
    for copy in copies:
        copy.wait()
    ids_ref, probs_ref, tok_ref, cot_ref = held
    tok_dev = tok_ref.shape[0]
    quarter = tok_ref.shape[1] // 4
    zh, c, yh = place_ref[0], place_ref[1], place_ref[2]
    upper = (
        lax.broadcasted_iota(jnp.int32, (tok_dev, tok_dev), 0)
        < lax.broadcasted_iota(jnp.int32, (tok_dev, tok_dev), 1)
    ).astype(BF16)
    ids = ids_ref[...]
    probs = probs_ref[...]
    place = lax.broadcasted_iota(jnp.int32, (2 * CAP, tok_dev), 0)
    tables = []
    for expert in (yh, 1 - yh):
        matches = ids == expert
        picked = jnp.any(matches, axis=0, keepdims=True)
        weight = jnp.sum(jnp.where(matches, probs, 0.0), axis=0, keepdims=True)
        flags = jnp.broadcast_to(jnp.where(picked, 1.0, 0.0), (2 * CAP, tok_dev))
        slot = jnp.dot(flags.astype(BF16), upper, preferred_element_type=F32).astype(jnp.int32)
        hot_rows = jnp.where((slot == place) & (place < CAP) & (flags > 0.5), 1.0, 0.0)
        hot_grads = jnp.where((slot == place - CAP) & (place >= CAP) & (flags > 0.5), 1.0, 0.0)
        row_weight = jnp.sum(hot_grads * weight, axis=1, keepdims=True)
        tables.append((hot_rows.astype(BF16), hot_grads.astype(BF16), row_weight))
    for half in range(2):
        for part in range(2):
            zone = (zh + half * (1 - 2 * zh)) * 2 + (c + part * (1 - 2 * c))
            lanes = pl.ds(pl.multiple_of(zone * quarter, quarter), quarter)
            tok = tok_ref[:, lanes]
            cot = cot_ref[:, lanes]
            base = (2 * half + part) * quarter
            for out, (hot_rows, hot_grads, row_weight) in zip((keep_ref, send_ref), tables, strict=True):
                rows = jnp.dot(hot_rows, tok, preferred_element_type=F32)
                grads = row_weight * jnp.dot(hot_grads, cot, preferred_element_type=F32)
                out[:, base : base + quarter] = (rows + grads).astype(BF16)


def fill_slots(place, ids, probs, tokens, cotangent):
    width = tokens.shape[1]
    vmem = pl.BlockSpec(memory_space=pltpu.VMEM)
    shape = jax.ShapeDtypeStruct((2 * CAP, width), BF16)
    return pl.pallas_call(
        slots_kernel,
        in_specs=[pl.BlockSpec(memory_space=pltpu.SMEM)] + [pl.BlockSpec(memory_space=pltpu.HBM)] * 4,
        out_specs=[vmem, vmem],
        out_shape=[shape, shape],
        scratch_shapes=[pltpu.VMEM(v.shape, v.dtype) for v in (ids, probs, tokens, cotangent)]
        + [pltpu.SemaphoreType.DMA] * 4,
        compiler_params=pltpu.CompilerParams(vmem_limit_bytes=VMEM_LIMIT),
    )(place, ids, probs, tokens, cotangent)


def assemble_kernel(*refs):
    *pieces, out_ref, wide_ref, total_ref = refs
    half = out_ref.shape[1] // 2
    at = 0
    for piece in pieces:
        count = piece.shape[0]
        wide_ref[:count, :] = piece[...].astype(F32)
        for j in range(0, count, 2 * CAP):
            total_ref[at : at + CAP, :half] = wide_ref[j : j + CAP, :]
            total_ref[at : at + CAP, half:] = wide_ref[j + CAP : j + 2 * CAP, :]
            at += CAP
    out_ref[...] = total_ref[...].astype(BF16)


def assemble(*pieces):
    half = pieces[0].shape[1]
    vmem = pl.BlockSpec(memory_space=pltpu.VMEM)
    rows = sum(piece.shape[0] for piece in pieces) // 2
    most = max(piece.shape[0] for piece in pieces)
    return pl.pallas_call(
        assemble_kernel,
        in_specs=[vmem] * len(pieces),
        out_specs=vmem,
        out_shape=jax.ShapeDtypeStruct((rows, 2 * half), BF16),
        scratch_shapes=[pltpu.VMEM((most, half), F32), pltpu.VMEM((rows, 2 * half), F32)],
        compiler_params=pltpu.CompilerParams(vmem_limit_bytes=VMEM_LIMIT),
    )(*pieces)


def forward_kernel(*refs):
    *chunks, up_ref, down_ref, out_ref = refs
    rows, both = chunks[0].shape
    half = both // 2
    ffw = up_ref.shape[1]
    for at, ref in enumerate(chunks):
        pre = jnp.dot(ref[:, :half], up_ref[...], preferred_element_type=F32)
        back = lax.dot_general(
            ref[:, half:], down_ref[...], (((1,), (1,)), ((), ())), preferred_element_type=F32
        )
        out_ref[at * rows : (at + 1) * rows, :ffw] = pre.astype(BF16)
        out_ref[at * rows : (at + 1) * rows, ffw:] = back.astype(BF16)


def forward(up, down, *chunks):
    rows, _ = chunks[0].shape
    ffw = up.shape[1]
    vmem = pl.BlockSpec(memory_space=pltpu.VMEM)
    return pl.pallas_call(
        forward_kernel,
        in_specs=[vmem] * (len(chunks) + 2),
        out_specs=vmem,
        out_shape=jax.ShapeDtypeStruct((len(chunks) * rows, 2 * ffw), BF16),
        compiler_params=pltpu.CompilerParams(vmem_limit_bytes=VMEM_LIMIT),
    )(*chunks, up, down)


TRANSPOSED = (((0,), (0,)), ((), ()))


def finish_hidden(sizes, sums, rows, hid_ref, inn_ref):
    half = rows // 2
    at = 0
    for size, (own_ref, got_ref) in zip(sizes, sums, strict=True):
        ffw = own_ref.shape[1] // 2
        for k in range(size):
            place = slice(k * rows, (k + 1) * rows)

            def total(lanes, own_ref=own_ref, got_ref=got_ref, place=place):
                got = got_ref[place, lanes].astype(F32)
                return own_ref[place, lanes].astype(F32) + jnp.concatenate([got[half:], got[:half]], axis=0)

            pre = total(slice(0, ffw))
            gate = 1.0 / (1.0 + jnp.exp(-pre))
            if hid_ref is not None:
                hid_ref[at : at + rows, :] = (pre * gate).astype(BF16)
            if inn_ref is not None:
                back = total(slice(ffw, 2 * ffw))
                inn_ref[at : at + rows, :] = (back * (gate * (1.0 + pre * (1.0 - gate)))).astype(BF16)
            at += rows


def backward_kernel(sizes, fresh, tile, *refs):
    refs = list(refs)
    sums = [(refs.pop(0), refs.pop(0)) for _ in sizes]
    chunks = [refs.pop(0) for _ in range(sum(sizes))]
    if not fresh:
        up_in, down_in = refs.pop(0), refs.pop(0)
    up_ref, down_ref, hid_ref, inn_ref = refs
    rows, both = chunks[0].shape
    half = both // 2
    finish_hidden(sizes, sums, rows, hid_ref, inn_ref)
    for lane in range(0, half, tile):
        grad_up = None if fresh else up_in[lane : lane + tile, :]
        grad_down = None if fresh else down_in[:, lane : lane + tile]
        for k, chunk in enumerate(chunks):
            at = slice(k * rows, (k + 1) * rows)
            more_up = lax.dot_general(
                chunk[:, lane : lane + tile], inn_ref[at], TRANSPOSED, preferred_element_type=F32
            )
            more_down = lax.dot_general(
                hid_ref[at], chunk[:, half + lane : half + lane + tile], TRANSPOSED, preferred_element_type=F32
            )
            grad_up = more_up if grad_up is None else grad_up + more_up
            grad_down = more_down if grad_down is None else grad_down + more_down
        up_ref[lane : lane + tile, :] = grad_up
        down_ref[:, lane : lane + tile] = grad_down


def backward(groups, totals):
    rows, both = groups[0][2][0].shape
    half = both // 2
    ffw = groups[0][0].shape[1] // 2
    sizes = tuple(len(chunks) for _, _, chunks in groups)
    fresh = totals is None
    operands = [value for own, got, _ in groups for value in (own, got)]
    operands += [chunk for _, _, chunks in groups for chunk in chunks]
    aliases = {} if fresh else {len(operands): 0, len(operands) + 1: 1}
    operands += [] if fresh else list(totals)
    vmem = pl.BlockSpec(memory_space=pltpu.VMEM)
    return pl.pallas_call(
        functools.partial(backward_kernel, sizes, fresh, half // 4),
        in_specs=[vmem] * len(operands),
        out_specs=[vmem, vmem],
        out_shape=[jax.ShapeDtypeStruct((half, ffw), F32), jax.ShapeDtypeStruct((ffw, half), F32)],
        scratch_shapes=[pltpu.VMEM((sum(sizes) * rows, ffw), BF16)] * 2,
        input_output_aliases=aliases,
        compiler_params=pltpu.CompilerParams(vmem_limit_bytes=VMEM_LIMIT),
    )(*operands)


def last_kernel(sizes, is_up, part, tile, added, *refs):
    refs = list(refs)
    sums = [(refs.pop(0), refs.pop(0)) for _ in sizes]
    chunks = [refs.pop(0) for _ in range(sum(sizes))]
    total_ref = refs.pop(0)
    add_ref = refs.pop(0) if added else None
    out_ref, mid_ref = refs
    rows, both = chunks[0].shape
    half = both // 2
    if is_up:
        finish_hidden(sizes, sums, rows, None, mid_ref)
    else:
        finish_hidden(sizes, sums, rows, mid_ref, None)
    for lane in range(0, half // 2, tile):
        source = part * (half // 2) + lane
        near = slice(lane, lane + tile)
        if is_up:
            grad = total_ref[source : source + tile, :]
        else:
            grad = total_ref[:, source : source + tile]
        for k, chunk in enumerate(chunks):
            at = slice(k * rows, (k + 1) * rows)
            if is_up:
                grad += lax.dot_general(
                    chunk[:, source : source + tile], mid_ref[at], TRANSPOSED, preferred_element_type=F32
                )
            else:
                lanes = slice(half + source, half + source + tile)
                grad += lax.dot_general(mid_ref[at], chunk[:, lanes], TRANSPOSED, preferred_element_type=F32)
        if is_up:
            grad = grad if add_ref is None else grad + add_ref[near, :].astype(F32)
            out_ref[near, :] = grad.astype(BF16)
        else:
            grad = grad if add_ref is None else grad + add_ref[:, near].astype(F32)
            out_ref[:, near] = grad.astype(BF16)


def last(groups, total, is_up, part, added=None):
    rows, both = groups[0][2][0].shape
    half = both // 2
    ffw = groups[0][0].shape[1] // 2
    sizes = tuple(len(chunks) for _, _, chunks in groups)
    operands = [value for own, got, _ in groups for value in (own, got)]
    operands += [chunk for _, _, chunks in groups for chunk in chunks]
    operands.append(total)
    if added is not None:
        operands.append(added)
    vmem = pl.BlockSpec(memory_space=pltpu.VMEM)
    shape = (half // 2, ffw) if is_up else (ffw, half // 2)
    return pl.pallas_call(
        functools.partial(last_kernel, sizes, is_up, part, half // 4, added is not None),
        in_specs=[vmem] * len(operands),
        out_specs=vmem,
        out_shape=jax.ShapeDtypeStruct(shape, BF16),
        scratch_shapes=[pltpu.VMEM((sum(sizes) * rows, ffw), BF16)],
        compiler_params=pltpu.CompilerParams(vmem_limit_bytes=VMEM_LIMIT),
    )(*operands)


def ring(value, axis, by):
    count = lax.axis_size(axis)
    return lax.ppermute(value, axis, [(i, (i + by) % count) for i in range(count)])


def along_z(value, by, cross, over=0):
    count = lax.axis_size("zl")

    def at(yh, zl, zh):
        return (yh * count + zl) * 2 + zh

    pairs = [
        (at(yh, zl, zh), at(yh ^ over, (zl + by) % count, zh ^ cross))
        for yh in range(2)
        for zl in range(count)
        for zh in range(2)
    ]
    return lax.ppermute(value, ("yh", "zl", "zh"), pairs)


def swap(value):
    return ring(value, "zh", 1)


def body(tokens, expert_ids, gate_probs, w_up, w_down, cotangent):
    barrier = lax.optimization_barrier
    place = jnp.stack([lax.axis_index("zh"), lax.axis_index("c"), lax.axis_index("yh")]).astype(jnp.int32)
    keep, send = fill_slots(place, expert_ids.T, gate_probs.T, tokens, cotangent)
    half = tokens.shape[1] // 2
    keep, send, up_c, down_c = barrier((keep, send, ring(w_up, "c", 1), ring(w_down, "c", 1)))
    k_mine, k_other = keep[:, :half], keep[:, half:]

    got = ring(send, "yh", 1)
    ks2, kc0, kc2 = along_z(k_mine, 2, 0), along_z(k_other, 0, 1), along_z(k_other, 2, 1)
    g_mine, g_other = got[:, :half], got[:, half:]
    s_mine, s_other = send[:, :half], send[:, half:]
    gs2, gc0, gc2 = along_z(s_mine, 2, 0, 1), along_z(s_other, 0, 1, 1), along_z(s_other, 2, 1, 1)
    mine = jnp.concatenate([k_mine, g_mine], axis=0)
    other = jnp.concatenate([k_other, g_other], axis=0)
    up = jnp.concatenate([w_up, up_c], axis=0)
    down = jnp.concatenate([w_down, down_c], axis=1)
    ks2, kc0, kc2, gs2, gc0, gc2, mine, other, up, down = barrier(
        (ks2, kc0, kc2, gs2, gc0, gc2, mine, other, up, down)
    )
    h1 = assemble(mine, ks2, gs2, kc0, gc0, kc2, gc2)
    h1, mine, other = barrier((h1, mine, other))

    s1, s3, c1, c3 = along_z(mine, 1, 0), along_z(mine, 3, 0), along_z(other, 1, 1), along_z(other, 3, 1)
    h1y, h1l = ring(h1, "yl", 1), ring(h1, "x", 1)
    own0 = forward(up, down, h1)
    s1, s3, c1, c3, h1, h1y, h1l, own0 = barrier((s1, s3, c1, c3, h1, h1y, h1l, own0))
    h2 = assemble(s1, s3, c1, c3)
    h2, h1, h1y, h1l, own0 = barrier((h2, h1, h1y, h1l, own0))

    h2y, h2l, h2r = ring(h2, "yl", 1), ring(h2, "x", 1), ring(h2, "x", -1)
    got0 = swap(own0)
    own1 = forward(up, down, h1y, h1l)
    got1 = swap(own1)
    own2 = forward(up, down, h2)
    h1, h1y, h1l, h2, h2y, h2l, h2r, own0, got0, own1, got1, own2 = barrier(
        (h1, h1y, h1l, h2, h2y, h2l, h2r, own0, got0, own1, got1, own2)
    )

    h2ly, h1yl, h1r = ring(h2l, "yl", 1), ring(h1y, "x", 1), ring(h1, "x", -1)
    got2 = swap(own2)
    own3 = forward(up, down, h2y, h2l)
    got3 = swap(own3)
    totals = backward([(own0, got0, (h1,)), (own1, got1, (h1y, h1l))], None)
    own4 = forward(up, down, h2r)
    h1y, h1l, h2, h2y, h2l, h2r, h2ly, h1yl, h1r, own2, got2, own3, got3, own4, totals = barrier(
        (h1y, h1l, h2, h2y, h2l, h2r, h2ly, h1yl, h1r, own2, got2, own3, got3, own4, totals)
    )

    h2ry, h2o, h1yr = ring(h2r, "yl", 1), ring(h2l, "x", 1), ring(h1y, "x", -1)
    got4 = swap(own4)
    own5 = forward(up, down, h2ly, h1yl)
    got5 = swap(own5)
    totals = backward([(own2, got2, (h2,)), (own3, got3, (h2y, h2l))], totals)
    own6 = forward(up, down, h1r)
    h1l, h2r, h2ly, h1yl, h1r, h2ry, h2o, h1yr, own4, got4, own5, got5, own6, totals = barrier(
        (h1l, h2r, h2ly, h1yl, h1r, h2ry, h2o, h1yr, own4, got4, own5, got5, own6, totals)
    )

    h2oy, h1o, h1yo = ring(h2o, "yl", 1), ring(h1l, "x", 1), ring(h1yr, "x", -1)
    got6 = swap(own6)
    own7 = forward(up, down, h2ry, h2o)
    got7 = swap(own7)
    totals = backward([(own4, got4, (h2r,)), (own5, got5, (h2ly, h1yl))], totals)
    own8 = forward(up, down, h1yr)
    h1r, h2ry, h2o, h1yr, h2oy, h1o, h1yo, own6, got6, own7, got7, own8, totals = barrier(
        (h1r, h2ry, h2o, h1yr, h2oy, h1o, h1yo, own6, got6, own7, got7, own8, totals)
    )

    got8 = swap(own8)
    own9 = forward(up, down, h2oy)
    got9 = swap(own9)
    own10 = forward(up, down, h1o, h1yo)
    got10 = swap(own10)
    totals = backward([(own6, got6, (h1r,)), (own7, got7, (h2ry, h2o))], totals)
    groups = [(own8, got8, (h1yr,)), (own9, got9, (h2oy,)), (own10, got10, (h1o, h1yo))]
    far_up = ring(last(groups, totals[0], True, 1), "c", 1)
    far_down = ring(last(groups, totals[1], False, 1), "c", 1)
    return last(groups, totals[0], True, 0, far_up), last(groups, totals[1], False, 0, far_down)


def solution(mesh):
    fine = Mesh(mesh.devices.reshape(2, 2, 4, 4, 2, 2), AXES)
    ep, fsdp = AXES[:4], AXES[4:]
    rows = P(AXES, None)
    return jax.shard_map(
        body,
        mesh=fine,
        in_specs=(rows, rows, rows, P(fsdp, ep), P(ep, fsdp), rows),
        out_specs=(P(fsdp, ep), P(ep, fsdp)),
        check_vma=False,
    )
```

```python
import functools

import jax
import jax.numpy as jnp
from jax import lax
from jax.experimental import pallas as pl
from jax.experimental.pallas import tpu as pltpu
from jax.sharding import Mesh
from jax.sharding import PartitionSpec as P

CAP = 18
AXES = ("yh", "yl", "zl", "x", "zh", "c")
F32 = jnp.float32
BF16 = jnp.bfloat16
VMEM_LIMIT = 32 * 1024 * 1024


def slots_kernel(place_ref, *refs):
    sources, outs, held, sems = refs[:4], refs[4:9], refs[9:13], refs[13:]
    mine_ref, other_ref, s_mine_ref, s_other_ref, send_ref = outs
    copies = [
        pltpu.make_async_copy(src, dst, sem) for src, dst, sem in zip(sources, held, sems, strict=True)
    ]
    for copy in copies:
        copy.start()
    for copy in copies:
        copy.wait()
    ids_ref, probs_ref, tok_ref, cot_ref = held
    tok_dev = tok_ref.shape[0]
    quarter = tok_ref.shape[1] // 4
    count = 4 * CAP
    zh, c, yh = place_ref[0], place_ref[1], place_ref[2]
    upper = (
        lax.broadcasted_iota(jnp.int32, (tok_dev, tok_dev), 0)
        < lax.broadcasted_iota(jnp.int32, (tok_dev, tok_dev), 1)
    ).astype(BF16)
    ids = ids_ref[...]
    probs = probs_ref[...]
    place = lax.broadcasted_iota(jnp.int32, (count, tok_dev), 0)
    tables = []
    for expert in (yh, 1 - yh):
        matches = ids == expert
        picked = jnp.any(matches, axis=0, keepdims=True)
        weight = jnp.sum(jnp.where(matches, probs, 0.0), axis=0, keepdims=True)
        flags = jnp.broadcast_to(jnp.where(picked, 1.0, 0.0), (count, tok_dev))
        slot = jnp.dot(flags.astype(BF16), upper, preferred_element_type=F32).astype(jnp.int32)

        def hot(first, slot=slot, flags=flags):
            inside = (place >= first) & (place < first + CAP)
            return jnp.where((slot == place - first) & inside & (flags > 0.5), 1.0, 0.0)

        parts = []
        for part in range(2):
            hot_grads = hot((2 * part + 1) * CAP)
            row_weight = jnp.sum(hot_grads * weight, axis=1, keepdims=True)
            parts.append((hot(2 * part * CAP).astype(BF16), hot_grads.astype(BF16), row_weight))
        tables.append(parts)
    for half in range(2):
        totals = [None, None]
        for part in range(2):
            zone = (zh + half * (1 - 2 * zh)) * 2 + (c + part * (1 - 2 * c))
            lanes = pl.ds(pl.multiple_of(zone * quarter, quarter), quarter)
            tok = tok_ref[:, lanes]
            cot = cot_ref[:, lanes]
            for k in range(2):
                hot_rows, hot_grads, row_weight = tables[k][part]
                more = jnp.dot(hot_rows, tok, preferred_element_type=F32)
                more += row_weight * jnp.dot(hot_grads, cot, preferred_element_type=F32)
                totals[k] = more if totals[k] is None else totals[k] + more
        (mine_ref, other_ref)[half][...] = totals[0].astype(BF16)
        (s_mine_ref, s_other_ref)[half][...] = totals[1].astype(BF16)
        send_ref[half] = totals[1].astype(BF16)


def fill_slots(place, ids, probs, tokens, cotangent):
    quarter = tokens.shape[1] // 4
    vmem = pl.BlockSpec(memory_space=pltpu.VMEM)
    shape = jax.ShapeDtypeStruct((4 * CAP, quarter), BF16)
    return pl.pallas_call(
        slots_kernel,
        in_specs=[pl.BlockSpec(memory_space=pltpu.SMEM)] + [pl.BlockSpec(memory_space=pltpu.HBM)] * 4,
        out_specs=[vmem] * 5,
        out_shape=[shape] * 4 + [jax.ShapeDtypeStruct((2, 4 * CAP, quarter), BF16)],
        scratch_shapes=[pltpu.VMEM(v.shape, v.dtype) for v in (ids, probs, tokens, cotangent)]
        + [pltpu.SemaphoreType.DMA] * 4,
        compiler_params=pltpu.CompilerParams(vmem_limit_bytes=VMEM_LIMIT),
    )(place, ids, probs, tokens, cotangent)


def assemble_kernel(*refs):
    *pieces, out_ref, wide_ref, total_ref = refs
    half = out_ref.shape[1] // 2
    quarter = half // 2
    at = 0
    for piece in pieces:
        count = piece.shape[0]
        wide_ref[:count, :] = piece[...].astype(F32)
        for j in range(0, count, 4 * CAP):
            for block, lane in enumerate((0, half, quarter, half + quarter)):
                source = j + block * CAP
                total_ref[at : at + CAP, lane : lane + quarter] = wide_ref[source : source + CAP, :]
            at += CAP
    out_ref[...] = total_ref[...].astype(BF16)


def assemble(*pieces):
    quarter = pieces[0].shape[1]
    vmem = pl.BlockSpec(memory_space=pltpu.VMEM)
    rows = sum(piece.shape[0] for piece in pieces) // 4
    most = max(piece.shape[0] for piece in pieces)
    return pl.pallas_call(
        assemble_kernel,
        in_specs=[vmem] * len(pieces),
        out_specs=vmem,
        out_shape=jax.ShapeDtypeStruct((rows, 4 * quarter), BF16),
        scratch_shapes=[pltpu.VMEM((most, quarter), F32), pltpu.VMEM((rows, 4 * quarter), F32)],
        compiler_params=pltpu.CompilerParams(vmem_limit_bytes=VMEM_LIMIT),
    )(*pieces)


def forward_kernel(*refs):
    *chunks, up_ref, down_ref, out_ref = refs
    rows, both = chunks[0].shape
    half = both // 2
    ffw = up_ref.shape[1]
    for at, ref in enumerate(chunks):
        pre = jnp.dot(ref[:, :half], up_ref[...], preferred_element_type=F32)
        back = lax.dot_general(
            ref[:, half:], down_ref[...], (((1,), (1,)), ((), ())), preferred_element_type=F32
        )
        out_ref[at * rows : (at + 1) * rows, :ffw] = pre.astype(BF16)
        out_ref[at * rows : (at + 1) * rows, ffw:] = back.astype(BF16)


def forward(up, down, *chunks):
    rows, _ = chunks[0].shape
    ffw = up.shape[1]
    vmem = pl.BlockSpec(memory_space=pltpu.VMEM)
    return pl.pallas_call(
        forward_kernel,
        in_specs=[vmem] * (len(chunks) + 2),
        out_specs=vmem,
        out_shape=jax.ShapeDtypeStruct((len(chunks) * rows, 2 * ffw), BF16),
        compiler_params=pltpu.CompilerParams(vmem_limit_bytes=VMEM_LIMIT),
    )(*chunks, up, down)


TRANSPOSED = (((0,), (0,)), ((), ()))


def finish_hidden(sizes, sums, rows, hid_ref, inn_ref):
    half = rows // 2
    at = 0
    for size, (own_ref, got_ref) in zip(sizes, sums, strict=True):
        ffw = own_ref.shape[1] // 2
        for k in range(size):
            place = slice(k * rows, (k + 1) * rows)

            def total(lanes, own_ref=own_ref, got_ref=got_ref, place=place):
                got = got_ref[place, lanes].astype(F32)
                return own_ref[place, lanes].astype(F32) + jnp.concatenate([got[half:], got[:half]], axis=0)

            pre = total(slice(0, ffw))
            gate = 1.0 / (1.0 + jnp.exp(-pre))
            if hid_ref is not None:
                hid_ref[at : at + rows, :] = (pre * gate).astype(BF16)
            if inn_ref is not None:
                back = total(slice(ffw, 2 * ffw))
                inn_ref[at : at + rows, :] = (back * (gate * (1.0 + pre * (1.0 - gate)))).astype(BF16)
            at += rows


def backward_kernel(sizes, fresh, tile, *refs):
    refs = list(refs)
    sums = [(refs.pop(0), refs.pop(0)) for _ in sizes]
    chunks = [refs.pop(0) for _ in range(sum(sizes))]
    if not fresh:
        up_in, down_in = refs.pop(0), refs.pop(0)
    up_ref, down_ref, hid_ref, inn_ref = refs
    rows, both = chunks[0].shape
    half = both // 2
    finish_hidden(sizes, sums, rows, hid_ref, inn_ref)
    for lane in range(0, half, tile):
        grad_up = None if fresh else up_in[lane : lane + tile, :]
        grad_down = None if fresh else down_in[:, lane : lane + tile]
        for k, chunk in enumerate(chunks):
            at = slice(k * rows, (k + 1) * rows)
            more_up = lax.dot_general(
                chunk[:, lane : lane + tile], inn_ref[at], TRANSPOSED, preferred_element_type=F32
            )
            more_down = lax.dot_general(
                hid_ref[at], chunk[:, half + lane : half + lane + tile], TRANSPOSED, preferred_element_type=F32
            )
            grad_up = more_up if grad_up is None else grad_up + more_up
            grad_down = more_down if grad_down is None else grad_down + more_down
        up_ref[lane : lane + tile, :] = grad_up
        down_ref[:, lane : lane + tile] = grad_down


def backward(groups, totals):
    rows, both = groups[0][2][0].shape
    half = both // 2
    ffw = groups[0][0].shape[1] // 2
    sizes = tuple(len(chunks) for _, _, chunks in groups)
    fresh = totals is None
    operands = [value for own, got, _ in groups for value in (own, got)]
    operands += [chunk for _, _, chunks in groups for chunk in chunks]
    aliases = {} if fresh else {len(operands): 0, len(operands) + 1: 1}
    operands += [] if fresh else list(totals)
    vmem = pl.BlockSpec(memory_space=pltpu.VMEM)
    return pl.pallas_call(
        functools.partial(backward_kernel, sizes, fresh, half // 4),
        in_specs=[vmem] * len(operands),
        out_specs=[vmem, vmem],
        out_shape=[jax.ShapeDtypeStruct((half, ffw), F32), jax.ShapeDtypeStruct((ffw, half), F32)],
        scratch_shapes=[pltpu.VMEM((sum(sizes) * rows, ffw), BF16)] * 2,
        input_output_aliases=aliases,
        compiler_params=pltpu.CompilerParams(vmem_limit_bytes=VMEM_LIMIT),
    )(*operands)


def last_kernel(sizes, is_up, part, tile, added, *refs):
    refs = list(refs)
    sums = [(refs.pop(0), refs.pop(0)) for _ in sizes]
    chunks = [refs.pop(0) for _ in range(sum(sizes))]
    total_ref = refs.pop(0)
    add_ref = refs.pop(0) if added else None
    out_ref, mid_ref = refs
    rows, both = chunks[0].shape
    half = both // 2
    if is_up:
        finish_hidden(sizes, sums, rows, None, mid_ref)
    else:
        finish_hidden(sizes, sums, rows, mid_ref, None)
    for lane in range(0, half // 2, tile):
        source = part * (half // 2) + lane
        near = slice(lane, lane + tile)
        if is_up:
            grad = total_ref[source : source + tile, :]
        else:
            grad = total_ref[:, source : source + tile]
        for k, chunk in enumerate(chunks):
            at = slice(k * rows, (k + 1) * rows)
            if is_up:
                grad += lax.dot_general(
                    chunk[:, source : source + tile], mid_ref[at], TRANSPOSED, preferred_element_type=F32
                )
            else:
                lanes = slice(half + source, half + source + tile)
                grad += lax.dot_general(mid_ref[at], chunk[:, lanes], TRANSPOSED, preferred_element_type=F32)
        if is_up:
            grad = grad if add_ref is None else grad + add_ref[near, :].astype(F32)
            out_ref[near, :] = grad.astype(BF16)
        else:
            grad = grad if add_ref is None else grad + add_ref[:, near].astype(F32)
            out_ref[:, near] = grad.astype(BF16)


def last(groups, total, is_up, part, added=None):
    rows, both = groups[0][2][0].shape
    half = both // 2
    ffw = groups[0][0].shape[1] // 2
    sizes = tuple(len(chunks) for _, _, chunks in groups)
    operands = [value for own, got, _ in groups for value in (own, got)]
    operands += [chunk for _, _, chunks in groups for chunk in chunks]
    operands.append(total)
    if added is not None:
        operands.append(added)
    vmem = pl.BlockSpec(memory_space=pltpu.VMEM)
    shape = (half // 2, ffw) if is_up else (ffw, half // 2)
    return pl.pallas_call(
        functools.partial(last_kernel, sizes, is_up, part, half // 4, added is not None),
        in_specs=[vmem] * len(operands),
        out_specs=vmem,
        out_shape=jax.ShapeDtypeStruct(shape, BF16),
        scratch_shapes=[pltpu.VMEM((sum(sizes) * rows, ffw), BF16)],
        compiler_params=pltpu.CompilerParams(vmem_limit_bytes=VMEM_LIMIT),
    )(*operands)


def ring(value, axis, by):
    count = lax.axis_size(axis)
    return lax.ppermute(value, axis, [(i, (i + by) % count) for i in range(count)])


def along_z(value, by, cross, over=0):
    count = lax.axis_size("zl")

    def at(yh, zl, zh):
        return (yh * count + zl) * 2 + zh

    pairs = [
        (at(yh, zl, zh), at(yh ^ over, (zl + by) % count, zh ^ cross))
        for yh in range(2)
        for zl in range(count)
        for zh in range(2)
    ]
    return lax.ppermute(value, ("yh", "zl", "zh"), pairs)


def swap(value):
    return ring(value, "zh", 1)


def body(tokens, expert_ids, gate_probs, w_up, w_down, cotangent):
    barrier = lax.optimization_barrier
    place = jnp.stack([lax.axis_index("zh"), lax.axis_index("c"), lax.axis_index("yh")]).astype(jnp.int32)
    k_mine, k_other, s_mine, s_other, send = fill_slots(
        place, expert_ids.T, gate_probs.T, tokens, cotangent
    )
    k_mine, k_other, s_mine, s_other, send, up_c, down_c = barrier(
        (k_mine, k_other, s_mine, s_other, send, ring(w_up, "c", 1), ring(w_down, "c", 1))
    )

    got = ring(send, "yh", 1)
    ks2, kc0, kc2 = along_z(k_mine, 2, 0), along_z(k_other, 0, 1), along_z(k_other, 2, 1)
    gs2, gc0, gc2 = along_z(s_mine, 2, 0, 1), along_z(s_other, 0, 1, 1), along_z(s_other, 2, 1, 1)
    mine = jnp.concatenate([k_mine, got[0]], axis=0)
    other = jnp.concatenate([k_other, got[1]], axis=0)
    up = jnp.concatenate([w_up, up_c], axis=0)
    down = jnp.concatenate([w_down, down_c], axis=1)
    ks2, kc0, kc2, gs2, gc0, gc2, mine, other, up, down = barrier(
        (ks2, kc0, kc2, gs2, gc0, gc2, mine, other, up, down)
    )
    h1 = assemble(mine, ks2, gs2, kc0, gc0, kc2, gc2)
    h1, mine, other = barrier((h1, mine, other))

    s1, s3, c1, c3 = along_z(mine, 1, 0), along_z(mine, 3, 0), along_z(other, 1, 1), along_z(other, 3, 1)
    h1y, h1l = ring(h1, "yl", 1), ring(h1, "x", 1)
    own0 = forward(up, down, h1)
    s1, s3, c1, c3, h1, h1y, h1l, own0 = barrier((s1, s3, c1, c3, h1, h1y, h1l, own0))
    h2 = assemble(s1, s3, c1, c3)
    h2, h1, h1y, h1l, own0 = barrier((h2, h1, h1y, h1l, own0))

    h2y, h2l, h2r = ring(h2, "yl", 1), ring(h2, "x", 1), ring(h2, "x", -1)
    got0 = swap(own0)
    own1 = forward(up, down, h1y, h1l)
    got1 = swap(own1)
    own2 = forward(up, down, h2)
    h1, h1y, h1l, h2, h2y, h2l, h2r, own0, got0, own1, got1, own2 = barrier(
        (h1, h1y, h1l, h2, h2y, h2l, h2r, own0, got0, own1, got1, own2)
    )

    h2ly, h1yl, h1r = ring(h2l, "yl", 1), ring(h1y, "x", 1), ring(h1, "x", -1)
    got2 = swap(own2)
    own3 = forward(up, down, h2y, h2l, h2r)
    got3 = swap(own3)
    totals = backward([(own0, got0, (h1,)), (own1, got1, (h1y, h1l))], None)
    h1y, h1l, h2, h2y, h2l, h2r, h2ly, h1yl, h1r, own2, got2, own3, got3, totals = barrier(
        (h1y, h1l, h2, h2y, h2l, h2r, h2ly, h1yl, h1r, own2, got2, own3, got3, totals)
    )

    h2ry, h2o, h1yr = ring(h2r, "yl", 1), ring(h2l, "x", 1), ring(h1y, "x", -1)
    own4 = forward(up, down, h2ly, h1yl)
    got4 = swap(own4)
    own5 = forward(up, down, h1r)
    got5 = swap(own5)
    totals = backward([(own2, got2, (h2,)), (own3, got3, (h2y, h2l, h2r))], totals)
    h1l, h2ly, h1yl, h1r, h2ry, h2o, h1yr, own4, got4, own5, got5, totals = barrier(
        (h1l, h2ly, h1yl, h1r, h2ry, h2o, h1yr, own4, got4, own5, got5, totals)
    )

    h2oy, h1o, h1yo = ring(h2o, "yl", 1), ring(h1l, "x", 1), ring(h1yr, "x", -1)
    own6 = forward(up, down, h2ry, h2o)
    got6 = swap(own6)
    own7 = forward(up, down, h1yr)
    got7 = swap(own7)
    totals = backward([(own4, got4, (h2ly, h1yl)), (own5, got5, (h1r,))], totals)
    h2ry, h2o, h1yr, h2oy, h1o, h1yo, own6, got6, own7, got7, totals = barrier(
        (h2ry, h2o, h1yr, h2oy, h1o, h1yo, own6, got6, own7, got7, totals)
    )

    own8 = forward(up, down, h2oy)
    got8 = swap(own8)
    own9 = forward(up, down, h1o, h1yo)
    got9 = swap(own9)
    totals = backward([(own6, got6, (h2ry, h2o)), (own7, got7, (h1yr,))], totals)
    groups = [(own8, got8, (h2oy,)), (own9, got9, (h1o, h1yo))]
    far_up = ring(last(groups, totals[0], True, 1), "c", 1)
    far_down = ring(last(groups, totals[1], False, 1), "c", 1)
    return last(groups, totals[0], True, 0, far_up), last(groups, totals[1], False, 0, far_down)


def solution(mesh):
    fine = Mesh(mesh.devices.reshape(2, 2, 4, 4, 2, 2), AXES)
    ep, fsdp = AXES[:4], AXES[4:]
    rows = P(AXES, None)
    return jax.shard_map(
        body,
        mesh=fine,
        in_specs=(rows, rows, rows, P(fsdp, ep), P(ep, fsdp), rows),
        out_specs=(P(fsdp, ep), P(ep, fsdp)),
        check_vma=False,
    )
```

```python
import functools

import jax
import jax.numpy as jnp
from jax import lax
from jax.experimental import pallas as pl
from jax.experimental.pallas import tpu as pltpu
from jax.sharding import Mesh
from jax.sharding import PartitionSpec as P

CAP = 18
AXES = ("yh", "yl", "zl", "x", "zh", "c")
F32 = jnp.float32
BF16 = jnp.bfloat16
VMEM_LIMIT = 32 * 1024 * 1024


def slots_kernel(place_ref, *refs):
    sources, outs, held, sems = refs[:4], refs[4:9], refs[9:13], refs[13:]
    mine_ref, other_ref, s_mine_ref, s_other_ref, send_ref = outs
    copies = [
        pltpu.make_async_copy(src, dst, sem) for src, dst, sem in zip(sources, held, sems, strict=True)
    ]
    for copy in copies:
        copy.start()
    for copy in copies:
        copy.wait()
    ids_ref, probs_ref, tok_ref, cot_ref = held
    tok_dev = tok_ref.shape[0]
    quarter = tok_ref.shape[1] // 4
    count = 4 * CAP
    zh, c, yh = place_ref[0], place_ref[1], place_ref[2]
    upper = (
        lax.broadcasted_iota(jnp.int32, (tok_dev, tok_dev), 0)
        < lax.broadcasted_iota(jnp.int32, (tok_dev, tok_dev), 1)
    ).astype(BF16)
    ids = ids_ref[...]
    probs = probs_ref[...]
    place = lax.broadcasted_iota(jnp.int32, (count, tok_dev), 0)
    tables = []
    for expert in (yh, 1 - yh):
        matches = ids == expert
        picked = jnp.any(matches, axis=0, keepdims=True)
        weight = jnp.sum(jnp.where(matches, probs, 0.0), axis=0, keepdims=True)
        flags = jnp.broadcast_to(jnp.where(picked, 1.0, 0.0), (count, tok_dev))
        slot = jnp.dot(flags.astype(BF16), upper, preferred_element_type=F32).astype(jnp.int32)

        def hot(first, slot=slot, flags=flags):
            inside = (place >= first) & (place < first + CAP)
            return jnp.where((slot == place - first) & inside & (flags > 0.5), 1.0, 0.0)

        parts = []
        for part in range(2):
            hot_grads = hot((2 * part + 1) * CAP)
            row_weight = jnp.sum(hot_grads * weight, axis=1, keepdims=True)
            parts.append((hot(2 * part * CAP).astype(BF16), hot_grads.astype(BF16), row_weight))
        tables.append(parts)
    for half in range(2):
        totals = [None, None]
        for part in range(2):
            zone = (zh + half * (1 - 2 * zh)) * 2 + (c + part * (1 - 2 * c))
            lanes = pl.ds(pl.multiple_of(zone * quarter, quarter), quarter)
            tok = tok_ref[:, lanes]
            cot = cot_ref[:, lanes]
            for k in range(2):
                hot_rows, hot_grads, row_weight = tables[k][part]
                more = jnp.dot(hot_rows, tok, preferred_element_type=F32)
                more += row_weight * jnp.dot(hot_grads, cot, preferred_element_type=F32)
                totals[k] = more if totals[k] is None else totals[k] + more
        (mine_ref, other_ref)[half][...] = totals[0].astype(BF16)
        (s_mine_ref, s_other_ref)[half][...] = totals[1].astype(BF16)
        send_ref[half] = totals[1].astype(BF16)


def fill_slots(place, ids, probs, tokens, cotangent):
    quarter = tokens.shape[1] // 4
    vmem = pl.BlockSpec(memory_space=pltpu.VMEM)
    shape = jax.ShapeDtypeStruct((4 * CAP, quarter), BF16)
    return pl.pallas_call(
        slots_kernel,
        in_specs=[pl.BlockSpec(memory_space=pltpu.SMEM)] + [pl.BlockSpec(memory_space=pltpu.HBM)] * 4,
        out_specs=[vmem] * 5,
        out_shape=[shape] * 4 + [jax.ShapeDtypeStruct((2, 4 * CAP, quarter), BF16)],
        scratch_shapes=[pltpu.VMEM(v.shape, v.dtype) for v in (ids, probs, tokens, cotangent)]
        + [pltpu.SemaphoreType.DMA] * 4,
        compiler_params=pltpu.CompilerParams(vmem_limit_bytes=VMEM_LIMIT),
    )(place, ids, probs, tokens, cotangent)


def assemble_kernel(*refs):
    *pieces, out_ref, wide_ref, total_ref = refs
    half = out_ref.shape[1] // 2
    quarter = half // 2
    at = 0
    for piece in pieces:
        count = piece.shape[0]
        wide_ref[:count, :] = piece[...].astype(F32)
        for j in range(0, count, 4 * CAP):
            for block, lane in enumerate((0, half, quarter, half + quarter)):
                source = j + block * CAP
                total_ref[at : at + CAP, lane : lane + quarter] = wide_ref[source : source + CAP, :]
            at += CAP
    out_ref[...] = total_ref[...].astype(BF16)


def assemble(*pieces):
    quarter = pieces[0].shape[1]
    vmem = pl.BlockSpec(memory_space=pltpu.VMEM)
    rows = sum(piece.shape[0] for piece in pieces) // 4
    most = max(piece.shape[0] for piece in pieces)
    return pl.pallas_call(
        assemble_kernel,
        in_specs=[vmem] * len(pieces),
        out_specs=vmem,
        out_shape=jax.ShapeDtypeStruct((rows, 4 * quarter), BF16),
        scratch_shapes=[pltpu.VMEM((most, quarter), F32), pltpu.VMEM((rows, 4 * quarter), F32)],
        compiler_params=pltpu.CompilerParams(vmem_limit_bytes=VMEM_LIMIT),
    )(*pieces)


def forward_kernel(*refs):
    *chunks, up_ref, down_ref, out_ref = refs
    rows, both = chunks[0].shape
    half = both // 2
    ffw = up_ref.shape[1]
    for at, ref in enumerate(chunks):
        pre = jnp.dot(ref[:, :half], up_ref[...], preferred_element_type=F32)
        back = lax.dot_general(
            ref[:, half:], down_ref[...], (((1,), (1,)), ((), ())), preferred_element_type=F32
        )
        out_ref[at * rows : (at + 1) * rows, :ffw] = pre.astype(BF16)
        out_ref[at * rows : (at + 1) * rows, ffw:] = back.astype(BF16)


def forward(up, down, *chunks):
    rows, _ = chunks[0].shape
    ffw = up.shape[1]
    vmem = pl.BlockSpec(memory_space=pltpu.VMEM)
    return pl.pallas_call(
        forward_kernel,
        in_specs=[vmem] * (len(chunks) + 2),
        out_specs=vmem,
        out_shape=jax.ShapeDtypeStruct((len(chunks) * rows, 2 * ffw), BF16),
        compiler_params=pltpu.CompilerParams(vmem_limit_bytes=VMEM_LIMIT),
    )(*chunks, up, down)


TRANSPOSED = (((0,), (0,)), ((), ()))


def finish_hidden(sizes, sums, rows, hid_ref, inn_ref):
    half = rows // 2
    at = 0
    for size, (own_ref, got_ref) in zip(sizes, sums, strict=True):
        ffw = own_ref.shape[1] // 2
        for k in range(size):
            place = slice(k * rows, (k + 1) * rows)

            def total(lanes, own_ref=own_ref, got_ref=got_ref, place=place):
                got = got_ref[place, lanes].astype(F32)
                return own_ref[place, lanes].astype(F32) + jnp.concatenate([got[half:], got[:half]], axis=0)

            pre = total(slice(0, ffw))
            gate = 1.0 / (1.0 + jnp.exp(-pre))
            if hid_ref is not None:
                hid_ref[at : at + rows, :] = (pre * gate).astype(BF16)
            if inn_ref is not None:
                back = total(slice(ffw, 2 * ffw))
                inn_ref[at : at + rows, :] = (back * (gate * (1.0 + pre * (1.0 - gate)))).astype(BF16)
            at += rows


def backward_kernel(sizes, fresh, tile, *refs):
    refs = list(refs)
    sums = [(refs.pop(0), refs.pop(0)) for _ in sizes]
    chunks = [refs.pop(0) for _ in range(sum(sizes))]
    if not fresh:
        up_in, down_in = refs.pop(0), refs.pop(0)
    up_ref, down_ref, hid_ref, inn_ref = refs
    rows, both = chunks[0].shape
    half = both // 2
    finish_hidden(sizes, sums, rows, hid_ref, inn_ref)
    for lane in range(0, half, tile):
        grad_up = None if fresh else up_in[lane : lane + tile, :]
        grad_down = None if fresh else down_in[:, lane : lane + tile]
        for k, chunk in enumerate(chunks):
            at = slice(k * rows, (k + 1) * rows)
            more_up = lax.dot_general(
                chunk[:, lane : lane + tile], inn_ref[at], TRANSPOSED, preferred_element_type=F32
            )
            more_down = lax.dot_general(
                hid_ref[at], chunk[:, half + lane : half + lane + tile], TRANSPOSED, preferred_element_type=F32
            )
            grad_up = more_up if grad_up is None else grad_up + more_up
            grad_down = more_down if grad_down is None else grad_down + more_down
        up_ref[lane : lane + tile, :] = grad_up
        down_ref[:, lane : lane + tile] = grad_down


def backward(groups, totals):
    rows, both = groups[0][2][0].shape
    half = both // 2
    ffw = groups[0][0].shape[1] // 2
    sizes = tuple(len(chunks) for _, _, chunks in groups)
    fresh = totals is None
    operands = [value for own, got, _ in groups for value in (own, got)]
    operands += [chunk for _, _, chunks in groups for chunk in chunks]
    aliases = {} if fresh else {len(operands): 0, len(operands) + 1: 1}
    operands += [] if fresh else list(totals)
    vmem = pl.BlockSpec(memory_space=pltpu.VMEM)
    return pl.pallas_call(
        functools.partial(backward_kernel, sizes, fresh, half // 4),
        in_specs=[vmem] * len(operands),
        out_specs=[vmem, vmem],
        out_shape=[jax.ShapeDtypeStruct((half, ffw), F32), jax.ShapeDtypeStruct((ffw, half), F32)],
        scratch_shapes=[pltpu.VMEM((sum(sizes) * rows, ffw), BF16)] * 2,
        input_output_aliases=aliases,
        compiler_params=pltpu.CompilerParams(vmem_limit_bytes=VMEM_LIMIT),
    )(*operands)


def last_kernel(sizes, is_up, part, tile, added, *refs):
    refs = list(refs)
    sums = [(refs.pop(0), refs.pop(0)) for _ in sizes]
    chunks = [refs.pop(0) for _ in range(sum(sizes))]
    total_ref = refs.pop(0)
    add_ref = refs.pop(0) if added else None
    out_ref, mid_ref = refs
    rows, both = chunks[0].shape
    half = both // 2
    if is_up:
        finish_hidden(sizes, sums, rows, None, mid_ref)
    else:
        finish_hidden(sizes, sums, rows, mid_ref, None)
    for lane in range(0, half // 2, tile):
        source = part * (half // 2) + lane
        near = slice(lane, lane + tile)
        if is_up:
            grad = total_ref[source : source + tile, :]
        else:
            grad = total_ref[:, source : source + tile]
        for k, chunk in enumerate(chunks):
            at = slice(k * rows, (k + 1) * rows)
            if is_up:
                grad += lax.dot_general(
                    chunk[:, source : source + tile], mid_ref[at], TRANSPOSED, preferred_element_type=F32
                )
            else:
                lanes = slice(half + source, half + source + tile)
                grad += lax.dot_general(mid_ref[at], chunk[:, lanes], TRANSPOSED, preferred_element_type=F32)
        if is_up:
            grad = grad if add_ref is None else grad + add_ref[near, :].astype(F32)
            out_ref[near, :] = grad.astype(BF16)
        else:
            grad = grad if add_ref is None else grad + add_ref[:, near].astype(F32)
            out_ref[:, near] = grad.astype(BF16)


def last(groups, total, is_up, part, added=None):
    rows, both = groups[0][2][0].shape
    half = both // 2
    ffw = groups[0][0].shape[1] // 2
    sizes = tuple(len(chunks) for _, _, chunks in groups)
    operands = [value for own, got, _ in groups for value in (own, got)]
    operands += [chunk for _, _, chunks in groups for chunk in chunks]
    operands.append(total)
    if added is not None:
        operands.append(added)
    vmem = pl.BlockSpec(memory_space=pltpu.VMEM)
    shape = (half // 2, ffw) if is_up else (ffw, half // 2)
    return pl.pallas_call(
        functools.partial(last_kernel, sizes, is_up, part, half // 4, added is not None),
        in_specs=[vmem] * len(operands),
        out_specs=vmem,
        out_shape=jax.ShapeDtypeStruct(shape, BF16),
        scratch_shapes=[pltpu.VMEM((sum(sizes) * rows, ffw), BF16)],
        compiler_params=pltpu.CompilerParams(vmem_limit_bytes=VMEM_LIMIT),
    )(*operands)


def ring(value, axis, by):
    count = lax.axis_size(axis)
    return lax.ppermute(value, axis, [(i, (i + by) % count) for i in range(count)])


def along_z(value, by, cross, over=0):
    count = lax.axis_size("zl")

    def at(yh, zl, zh):
        return (yh * count + zl) * 2 + zh

    pairs = [
        (at(yh, zl, zh), at(yh ^ over, (zl + by) % count, zh ^ cross))
        for yh in range(2)
        for zl in range(count)
        for zh in range(2)
    ]
    return lax.ppermute(value, ("yh", "zl", "zh"), pairs)


def swap(value):
    return ring(value, "zh", 1)


def body(tokens, expert_ids, gate_probs, w_up, w_down, cotangent):
    barrier = lax.optimization_barrier
    place = jnp.stack([lax.axis_index("zh"), lax.axis_index("c"), lax.axis_index("yh")]).astype(jnp.int32)
    k_mine, k_other, s_mine, s_other, send = fill_slots(
        place, expert_ids.T, gate_probs.T, tokens, cotangent
    )
    k_mine, k_other, s_mine, s_other, send, up_c, down_c = barrier(
        (k_mine, k_other, s_mine, s_other, send, ring(w_up, "c", 1), ring(w_down, "c", 1))
    )

    got = ring(send, "yh", 1)
    ks2, kc0, kc2 = along_z(k_mine, 2, 0), along_z(k_other, 0, 1), along_z(k_other, 2, 1)
    gs2, gc0, gc2 = along_z(s_mine, 2, 0, 1), along_z(s_other, 0, 1, 1), along_z(s_other, 2, 1, 1)
    mine = jnp.concatenate([k_mine, got[0]], axis=0)
    other = jnp.concatenate([k_other, got[1]], axis=0)
    up = jnp.concatenate([w_up, up_c], axis=0)
    down = jnp.concatenate([w_down, down_c], axis=1)
    ks2, kc0, kc2, gs2, gc0, gc2, mine, other, up, down = barrier(
        (ks2, kc0, kc2, gs2, gc0, gc2, mine, other, up, down)
    )
    h1 = assemble(mine, ks2, gs2, kc0, gc0, kc2, gc2)
    h1, mine, other = barrier((h1, mine, other))

    s1, s3, c1, c3 = along_z(mine, 1, 0), along_z(mine, 3, 0), along_z(other, 1, 1), along_z(other, 3, 1)
    h1y, h1l = ring(h1, "yl", 1), ring(h1, "x", 1)
    own0 = forward(up, down, h1)
    s1, s3, c1, c3, h1, h1y, h1l, own0 = barrier((s1, s3, c1, c3, h1, h1y, h1l, own0))
    h2 = assemble(s1, s3, c1, c3)
    h2, h1, h1y, h1l, own0 = barrier((h2, h1, h1y, h1l, own0))

    h2y, h2l, h2r = ring(h2, "yl", 1), ring(h2, "x", 1), ring(h2, "x", -1)
    got0 = swap(own0)
    own1 = forward(up, down, h1y, h1l)
    got1 = swap(own1)
    h1, h1y, h1l, h2, h2y, h2l, h2r, own0, got0, own1, got1 = barrier(
        (h1, h1y, h1l, h2, h2y, h2l, h2r, own0, got0, own1, got1)
    )

    h2ly, h1yl, h1r = ring(h2l, "yl", 1), ring(h1y, "x", 1), ring(h1, "x", -1)
    own2 = forward(up, down, h2, h2y, h2l, h2r)
    got2 = swap(own2)
    totals = backward([(own0, got0, (h1,)), (own1, got1, (h1y, h1l))], None)
    h1y, h1l, h2, h2y, h2l, h2r, h2ly, h1yl, h1r, own2, got2, totals = barrier(
        (h1y, h1l, h2, h2y, h2l, h2r, h2ly, h1yl, h1r, own2, got2, totals)
    )

    h2ry, h2o, h1yr = ring(h2r, "yl", 1), ring(h2l, "x", 1), ring(h1y, "x", -1)
    own3 = forward(up, down, h2ly, h1yl, h1r)
    got3 = swap(own3)
    totals = backward([(own2, got2, (h2, h2y, h2l, h2r))], totals)
    h1l, h2ly, h1yl, h1r, h2ry, h2o, h1yr, own3, got3, totals = barrier(
        (h1l, h2ly, h1yl, h1r, h2ry, h2o, h1yr, own3, got3, totals)
    )

    h2oy, h1o, h1yo = ring(h2o, "yl", 1), ring(h1l, "x", 1), ring(h1yr, "x", -1)
    own4 = forward(up, down, h2ry, h2o, h1yr)
    got4 = swap(own4)
    totals = backward([(own3, got3, (h2ly, h1yl, h1r))], totals)
    h2ry, h2o, h1yr, h2oy, h1o, h1yo, own4, got4, totals = barrier(
        (h2ry, h2o, h1yr, h2oy, h1o, h1yo, own4, got4, totals)
    )

    own5 = forward(up, down, h2oy, h1o, h1yo)
    got5 = swap(own5)
    totals = backward([(own4, got4, (h2ry, h2o, h1yr))], totals)
    groups = [(own5, got5, (h2oy, h1o, h1yo))]
    far_up = ring(last(groups, totals[0], True, 1), "c", 1)
    far_down = ring(last(groups, totals[1], False, 1), "c", 1)
    return last(groups, totals[0], True, 0, far_up), last(groups, totals[1], False, 0, far_down)


def solution(mesh):
    fine = Mesh(mesh.devices.reshape(2, 2, 4, 4, 2, 2), AXES)
    ep, fsdp = AXES[:4], AXES[4:]
    rows = P(AXES, None)
    return jax.shard_map(
        body,
        mesh=fine,
        in_specs=(rows, rows, rows, P(fsdp, ep), P(ep, fsdp), rows),
        out_specs=(P(fsdp, ep), P(ep, fsdp)),
        check_vma=False,
    )
```

```python
import functools

import jax
import jax.numpy as jnp
from jax import lax
from jax.experimental import pallas as pl
from jax.experimental.pallas import tpu as pltpu
from jax.sharding import Mesh
from jax.sharding import PartitionSpec as P

CAP = 18
AXES = ("yh", "yl", "zl", "x", "zh", "c")
F32 = jnp.float32
BF16 = jnp.bfloat16
VMEM_LIMIT = 32 * 1024 * 1024


def slots_kernel(place_ref, *refs):
    sources, outs, held, sems = refs[:4], refs[4:9], refs[9:13], refs[13:]
    mine_ref, other_ref, s_mine_ref, s_other_ref, send_ref = outs
    copies = [
        pltpu.make_async_copy(src, dst, sem) for src, dst, sem in zip(sources, held, sems, strict=True)
    ]
    for copy in copies:
        copy.start()
    for copy in copies:
        copy.wait()
    ids_ref, probs_ref, tok_ref, cot_ref = held
    tok_dev = tok_ref.shape[0]
    quarter = tok_ref.shape[1] // 4
    count = 4 * CAP
    zh, c, yh = place_ref[0], place_ref[1], place_ref[2]
    upper = (
        lax.broadcasted_iota(jnp.int32, (tok_dev, tok_dev), 0)
        < lax.broadcasted_iota(jnp.int32, (tok_dev, tok_dev), 1)
    ).astype(BF16)
    ids = ids_ref[...]
    probs = probs_ref[...]
    place = lax.broadcasted_iota(jnp.int32, (count, tok_dev), 0)
    tables = []
    for expert in (yh, 1 - yh):
        matches = ids == expert
        picked = jnp.any(matches, axis=0, keepdims=True)
        weight = jnp.sum(jnp.where(matches, probs, 0.0), axis=0, keepdims=True)
        flags = jnp.broadcast_to(jnp.where(picked, 1.0, 0.0), (count, tok_dev))
        slot = jnp.dot(flags.astype(BF16), upper, preferred_element_type=F32).astype(jnp.int32)

        def hot(first, slot=slot, flags=flags):
            inside = (place >= first) & (place < first + CAP)
            return jnp.where((slot == place - first) & inside & (flags > 0.5), 1.0, 0.0)

        parts = []
        for part in range(2):
            hot_grads = hot((2 * part + 1) * CAP)
            row_weight = jnp.sum(hot_grads * weight, axis=1, keepdims=True)
            parts.append((hot(2 * part * CAP).astype(BF16), hot_grads.astype(BF16), row_weight))
        tables.append(parts)
    for half in range(2):
        totals = [None, None]
        for part in range(2):
            zone = (zh + half * (1 - 2 * zh)) * 2 + (c + part * (1 - 2 * c))
            lanes = pl.ds(pl.multiple_of(zone * quarter, quarter), quarter)
            tok = tok_ref[:, lanes]
            cot = cot_ref[:, lanes]
            for k in range(2):
                hot_rows, hot_grads, row_weight = tables[k][part]
                more = jnp.dot(hot_rows, tok, preferred_element_type=F32)
                more += row_weight * jnp.dot(hot_grads, cot, preferred_element_type=F32)
                totals[k] = more if totals[k] is None else totals[k] + more
        (mine_ref, other_ref)[half][...] = totals[0].astype(BF16)
        (s_mine_ref, s_other_ref)[half][...] = totals[1].astype(BF16)
        send_ref[half] = totals[1].astype(BF16)


def fill_slots(place, ids, probs, tokens, cotangent):
    quarter = tokens.shape[1] // 4
    vmem = pl.BlockSpec(memory_space=pltpu.VMEM)
    shape = jax.ShapeDtypeStruct((4 * CAP, quarter), BF16)
    return pl.pallas_call(
        slots_kernel,
        in_specs=[pl.BlockSpec(memory_space=pltpu.SMEM)] + [pl.BlockSpec(memory_space=pltpu.HBM)] * 4,
        out_specs=[vmem] * 5,
        out_shape=[shape] * 4 + [jax.ShapeDtypeStruct((2, 4 * CAP, quarter), BF16)],
        scratch_shapes=[pltpu.VMEM(v.shape, v.dtype) for v in (ids, probs, tokens, cotangent)]
        + [pltpu.SemaphoreType.DMA] * 4,
        compiler_params=pltpu.CompilerParams(vmem_limit_bytes=VMEM_LIMIT),
    )(place, ids, probs, tokens, cotangent)


def assemble_kernel(*refs):
    *pieces, out_ref, wide_ref, total_ref = refs
    half = out_ref.shape[1] // 2
    quarter = half // 2
    at = 0
    for piece in pieces:
        count = piece.shape[0]
        wide_ref[:count, :] = piece[...].astype(F32)
        for j in range(0, count, 4 * CAP):
            for block, lane in enumerate((0, half, quarter, half + quarter)):
                source = j + block * CAP
                total_ref[at : at + CAP, lane : lane + quarter] = wide_ref[source : source + CAP, :]
            at += CAP
    out_ref[...] = total_ref[...].astype(BF16)


def assemble(*pieces):
    quarter = pieces[0].shape[1]
    vmem = pl.BlockSpec(memory_space=pltpu.VMEM)
    rows = sum(piece.shape[0] for piece in pieces) // 4
    most = max(piece.shape[0] for piece in pieces)
    return pl.pallas_call(
        assemble_kernel,
        in_specs=[vmem] * len(pieces),
        out_specs=vmem,
        out_shape=jax.ShapeDtypeStruct((rows, 4 * quarter), BF16),
        scratch_shapes=[pltpu.VMEM((most, quarter), F32), pltpu.VMEM((rows, 4 * quarter), F32)],
        compiler_params=pltpu.CompilerParams(vmem_limit_bytes=VMEM_LIMIT),
    )(*pieces)


def forward_kernel(*refs):
    *chunks, up_ref, down_ref, out_ref = refs
    rows, both = chunks[0].shape
    half = both // 2
    ffw = up_ref.shape[1]
    for at, ref in enumerate(chunks):
        pre = jnp.dot(ref[:, :half], up_ref[...], preferred_element_type=F32)
        back = lax.dot_general(
            ref[:, half:], down_ref[...], (((1,), (1,)), ((), ())), preferred_element_type=F32
        )
        out_ref[at * rows : (at + 1) * rows, :ffw] = pre.astype(BF16)
        out_ref[at * rows : (at + 1) * rows, ffw:] = back.astype(BF16)


def forward(up, down, *chunks):
    rows, _ = chunks[0].shape
    ffw = up.shape[1]
    vmem = pl.BlockSpec(memory_space=pltpu.VMEM)
    return pl.pallas_call(
        forward_kernel,
        in_specs=[vmem] * (len(chunks) + 2),
        out_specs=vmem,
        out_shape=jax.ShapeDtypeStruct((len(chunks) * rows, 2 * ffw), BF16),
        compiler_params=pltpu.CompilerParams(vmem_limit_bytes=VMEM_LIMIT),
    )(*chunks, up, down)


TRANSPOSED = (((0,), (0,)), ((), ()))


def finish_hidden(sizes, sums, rows, hid_ref, inn_ref):
    half = rows // 2
    at = 0
    for size, (own_ref, got_ref) in zip(sizes, sums, strict=True):
        ffw = own_ref.shape[1] // 2
        for k in range(size):
            place = slice(k * rows, (k + 1) * rows)

            def total(lanes, own_ref=own_ref, got_ref=got_ref, place=place):
                got = got_ref[place, lanes].astype(F32)
                return own_ref[place, lanes].astype(F32) + jnp.concatenate([got[half:], got[:half]], axis=0)

            pre = total(slice(0, ffw))
            gate = 1.0 / (1.0 + jnp.exp(-pre))
            if hid_ref is not None:
                hid_ref[at : at + rows, :] = (pre * gate).astype(BF16)
            if inn_ref is not None:
                back = total(slice(ffw, 2 * ffw))
                inn_ref[at : at + rows, :] = (back * (gate * (1.0 + pre * (1.0 - gate)))).astype(BF16)
            at += rows


def backward_kernel(sizes, fresh, tile, *refs):
    refs = list(refs)
    sums = [(refs.pop(0), refs.pop(0)) for _ in sizes]
    chunks = [refs.pop(0) for _ in range(sum(sizes))]
    if not fresh:
        up_in, down_in = refs.pop(0), refs.pop(0)
    up_ref, down_ref, hid_ref, inn_ref = refs
    rows, both = chunks[0].shape
    half = both // 2
    finish_hidden(sizes, sums, rows, hid_ref, inn_ref)
    for lane in range(0, half, tile):
        grad_up = None if fresh else up_in[lane : lane + tile, :]
        grad_down = None if fresh else down_in[:, lane : lane + tile]
        for k, chunk in enumerate(chunks):
            at = slice(k * rows, (k + 1) * rows)
            more_up = lax.dot_general(
                chunk[:, lane : lane + tile], inn_ref[at], TRANSPOSED, preferred_element_type=F32
            )
            more_down = lax.dot_general(
                hid_ref[at], chunk[:, half + lane : half + lane + tile], TRANSPOSED, preferred_element_type=F32
            )
            grad_up = more_up if grad_up is None else grad_up + more_up
            grad_down = more_down if grad_down is None else grad_down + more_down
        up_ref[lane : lane + tile, :] = grad_up
        down_ref[:, lane : lane + tile] = grad_down


def backward(groups, totals):
    rows, both = groups[0][2][0].shape
    half = both // 2
    ffw = groups[0][0].shape[1] // 2
    sizes = tuple(len(chunks) for _, _, chunks in groups)
    fresh = totals is None
    operands = [value for own, got, _ in groups for value in (own, got)]
    operands += [chunk for _, _, chunks in groups for chunk in chunks]
    aliases = {} if fresh else {len(operands): 0, len(operands) + 1: 1}
    operands += [] if fresh else list(totals)
    vmem = pl.BlockSpec(memory_space=pltpu.VMEM)
    return pl.pallas_call(
        functools.partial(backward_kernel, sizes, fresh, half // 4),
        in_specs=[vmem] * len(operands),
        out_specs=[vmem, vmem],
        out_shape=[jax.ShapeDtypeStruct((half, ffw), F32), jax.ShapeDtypeStruct((ffw, half), F32)],
        scratch_shapes=[pltpu.VMEM((sum(sizes) * rows, ffw), BF16)] * 2,
        input_output_aliases=aliases,
        compiler_params=pltpu.CompilerParams(vmem_limit_bytes=VMEM_LIMIT),
    )(*operands)


def last_kernel(sizes, is_up, part, tile, added, *refs):
    refs = list(refs)
    sums = [(refs.pop(0), refs.pop(0)) for _ in sizes]
    chunks = [refs.pop(0) for _ in range(sum(sizes))]
    total_ref = refs.pop(0)
    add_ref = refs.pop(0) if added else None
    out_ref, mid_ref = refs
    rows, both = chunks[0].shape
    half = both // 2
    if is_up:
        finish_hidden(sizes, sums, rows, None, mid_ref)
    else:
        finish_hidden(sizes, sums, rows, mid_ref, None)
    for lane in range(0, half // 2, tile):
        source = part * (half // 2) + lane
        near = slice(lane, lane + tile)
        if is_up:
            grad = total_ref[source : source + tile, :]
        else:
            grad = total_ref[:, source : source + tile]
        for k, chunk in enumerate(chunks):
            at = slice(k * rows, (k + 1) * rows)
            if is_up:
                grad += lax.dot_general(
                    chunk[:, source : source + tile], mid_ref[at], TRANSPOSED, preferred_element_type=F32
                )
            else:
                lanes = slice(half + source, half + source + tile)
                grad += lax.dot_general(mid_ref[at], chunk[:, lanes], TRANSPOSED, preferred_element_type=F32)
        if is_up:
            grad = grad if add_ref is None else grad + add_ref[near, :].astype(F32)
            out_ref[near, :] = grad.astype(BF16)
        else:
            grad = grad if add_ref is None else grad + add_ref[:, near].astype(F32)
            out_ref[:, near] = grad.astype(BF16)


def last(groups, total, is_up, part, added=None):
    rows, both = groups[0][2][0].shape
    half = both // 2
    ffw = groups[0][0].shape[1] // 2
    sizes = tuple(len(chunks) for _, _, chunks in groups)
    operands = [value for own, got, _ in groups for value in (own, got)]
    operands += [chunk for _, _, chunks in groups for chunk in chunks]
    operands.append(total)
    if added is not None:
        operands.append(added)
    vmem = pl.BlockSpec(memory_space=pltpu.VMEM)
    shape = (half // 2, ffw) if is_up else (ffw, half // 2)
    return pl.pallas_call(
        functools.partial(last_kernel, sizes, is_up, part, half // 4, added is not None),
        in_specs=[vmem] * len(operands),
        out_specs=vmem,
        out_shape=jax.ShapeDtypeStruct(shape, BF16),
        scratch_shapes=[pltpu.VMEM((sum(sizes) * rows, ffw), BF16)],
        compiler_params=pltpu.CompilerParams(vmem_limit_bytes=VMEM_LIMIT),
    )(*operands)


def ring(value, axis, by):
    count = lax.axis_size(axis)
    return lax.ppermute(value, axis, [(i, (i + by) % count) for i in range(count)])


def along_z(value, by, cross, over=0):
    count = lax.axis_size("zl")

    def at(yh, zl, zh):
        return (yh * count + zl) * 2 + zh

    pairs = [
        (at(yh, zl, zh), at(yh ^ over, (zl + by) % count, zh ^ cross))
        for yh in range(2)
        for zl in range(count)
        for zh in range(2)
    ]
    return lax.ppermute(value, ("yh", "zl", "zh"), pairs)


def swap(value):
    return ring(value, "zh", 1)


def body(tokens, expert_ids, gate_probs, w_up, w_down, cotangent):
    barrier = lax.optimization_barrier
    place = jnp.stack([lax.axis_index("zh"), lax.axis_index("c"), lax.axis_index("yh")]).astype(jnp.int32)
    k_mine, k_other, s_mine, s_other, send = fill_slots(
        place, expert_ids.T, gate_probs.T, tokens, cotangent
    )
    k_mine, k_other, s_mine, s_other, send, up_c, down_c = barrier(
        (k_mine, k_other, s_mine, s_other, send, ring(w_up, "c", 1), ring(w_down, "c", 1))
    )

    got = ring(send, "yh", 1)
    ks2, kc0, kc2 = along_z(k_mine, 2, 0), along_z(k_other, 0, 1), along_z(k_other, 2, 1)
    gs2, gc0, gc2 = along_z(s_mine, 2, 0, 1), along_z(s_other, 0, 1, 1), along_z(s_other, 2, 1, 1)
    mine = jnp.concatenate([k_mine, got[0]], axis=0)
    other = jnp.concatenate([k_other, got[1]], axis=0)
    up = jnp.concatenate([w_up, up_c], axis=0)
    down = jnp.concatenate([w_down, down_c], axis=1)
    ks2, kc0, kc2, gs2, gc0, gc2, mine, other, up, down = barrier(
        (ks2, kc0, kc2, gs2, gc0, gc2, mine, other, up, down)
    )
    h1 = assemble(mine, ks2, gs2, kc0, gc0, kc2, gc2)
    h1, mine, other = barrier((h1, mine, other))

    s1, s3, c1, c3 = along_z(mine, 1, 0), along_z(mine, 3, 0), along_z(other, 1, 1), along_z(other, 3, 1)
    h1y, h1l = ring(h1, "yl", 1), ring(h1, "x", 1)
    own0 = forward(up, down, h1)
    s1, s3, c1, c3, h1, h1y, h1l, own0 = barrier((s1, s3, c1, c3, h1, h1y, h1l, own0))
    h2 = assemble(s1, s3, c1, c3)
    h2, h1, h1y, h1l, own0 = barrier((h2, h1, h1y, h1l, own0))

    h2y, h2l, h2r = ring(h2, "yl", 1), ring(h2, "x", 1), ring(h2, "x", -1)
    got0 = swap(own0)
    own1 = forward(up, down, h1y, h1l)
    got1 = swap(own1)
    h1, h1y, h1l, h2, h2y, h2l, h2r, own0, got0, own1, got1 = barrier(
        (h1, h1y, h1l, h2, h2y, h2l, h2r, own0, got0, own1, got1)
    )

    h2ly, h1yl, h1r = ring(h2l, "yl", 1), ring(h1y, "x", 1), ring(h1, "x", -1)
    own2 = forward(up, down, h2, h2y, h2l, h2r)
    got2 = swap(own2)
    totals = backward([(own0, got0, (h1,)), (own1, got1, (h1y, h1l))], None)
    h1y, h1l, h2, h2y, h2l, h2r, h2ly, h1yl, h1r, own2, got2, totals = barrier(
        (h1y, h1l, h2, h2y, h2l, h2r, h2ly, h1yl, h1r, own2, got2, totals)
    )

    h2ry, h2o, h1yr = ring(h2r, "yl", 1), ring(h2l, "x", 1), ring(h1y, "x", -1)
    own3 = forward(up, down, h2ly, h1yl, h1r)
    got3 = swap(own3)
    totals = backward([(own2, got2, (h2, h2y, h2l, h2r))], totals)
    h1l, h2ly, h1yl, h1r, h2ry, h2o, h1yr, own3, got3, totals = barrier(
        (h1l, h2ly, h1yl, h1r, h2ry, h2o, h1yr, own3, got3, totals)
    )

    h2oy, h1o, h1yo = ring(h2o, "yl", 1), ring(h1l, "x", 1), ring(h1yr, "x", -1)
    own4 = forward(up, down, h2ry, h2o, h1yr)
    got4 = swap(own4)
    totals = backward([(own3, got3, (h2ly, h1yl, h1r))], totals)
    h2ry, h2o, h1yr, h2oy, h1o, h1yo, own4, got4, totals = barrier(
        (h2ry, h2o, h1yr, h2oy, h1o, h1yo, own4, got4, totals)
    )

    own5 = forward(up, down, h2oy)
    got5 = swap(own5)
    own6 = forward(up, down, h1o, h1yo)
    got6 = swap(own6)
    totals = backward([(own4, got4, (h2ry, h2o, h1yr))], totals)
    groups = [(own5, got5, (h2oy,)), (own6, got6, (h1o, h1yo))]
    far_up = ring(last(groups, totals[0], True, 1), "c", 1)
    far_down = ring(last(groups, totals[1], False, 1), "c", 1)
    return last(groups, totals[0], True, 0, far_up), last(groups, totals[1], False, 0, far_down)


def solution(mesh):
    fine = Mesh(mesh.devices.reshape(2, 2, 4, 4, 2, 2), AXES)
    ep, fsdp = AXES[:4], AXES[4:]
    rows = P(AXES, None)
    return jax.shard_map(
        body,
        mesh=fine,
        in_specs=(rows, rows, rows, P(fsdp, ep), P(ep, fsdp), rows),
        out_specs=(P(fsdp, ep), P(ep, fsdp)),
        check_vma=False,
    )
```
